32 devices in a mesh: seq: 8 (over y, x, core), head: 4 (over z).
Axes of the slice: x: 2, y: 2, z: 4, core: 2. Of those that a mesh axis runs over, the one named last changes fastest.
Arguments:
- qk: bfloat16 [16384, 2048], P('seq', 'head'), may hold values from -480 to 480, as said below
- values: bfloat16 [16384, 2048], P('seq', 'head'), may hold values from -6 to 6
- bucket: int32 [64, 16], replicated, may hold values from 0 to 1
- pair_row: int32 [8, 8, 3], P('seq'), may hold values from 0 to 7, as said below
- pair_col: int32 [8, 8, 3], P('seq'), may hold values from 0 to 7, as said below
- pair_count: int32 [8, 8], P('seq'), may hold values from 0 to 3, as said below
- w_out: bfloat16 [2048, 2048], P('head'), may hold values from -0.125 to 0.125
Outputs:
- projected: bfloat16 [16384, 2048], P(('seq', 'head'))
The draws below stay inside these ranges and needn't reach their ends.
Inputs may be any that keep to these rules, and one draw needn't show every extreme that they name: `pair_row`: every value is a local block index of the shard it refers to. `pair_col`: every value is a local block index; a pair never joins a block with itself. `pair_count`: some shard has 3 live slots towards every shard in every draw. `qk`: row scales of the vectors may differ widely.
All inputs are finite; a program needn't handle non-finite values.
Results may differ from the reference program's by a relative error of at most 0.014.
Values may be sent and summed in bfloat16 or wider, within the bound.
No kernel may reach another device: no remote copies, remote signals or barrier semaphores. Data moves between devices by JAX's collectives and lax.ppermute only.
A program may use at most 128 MiB of HBM per device.

```python
import math
import jax
import jax.numpy as jnp
from jax import lax

D = 2048
H = 16
HD = 128
BLOCK = 256
NBUCK = 2
BPD = 8
PAIR_CAP = 3
NSHARD = 8
TOKENS = 16384
NBLK = 64


def pair_tables(key):
    base_key = jax.random.fold_in(key, 7)
    key_rows, key_cols, key_count, key_phase = jax.random.split(base_key, 4)
    rows = jax.random.randint(key_rows, (NSHARD, NSHARD, PAIR_CAP), 0, BPD, dtype=jnp.int32)
    cols = jax.random.randint(key_cols, (NSHARD, NSHARD, PAIR_CAP), 0, BPD, dtype=jnp.int32)
    shard_ids = jnp.arange(NSHARD, dtype=jnp.int32)
    same = (shard_ids[:, None, None] == shard_ids[None, :, None]) & (rows == cols)
    cols = jnp.where(same, (cols + 1) % BPD, cols)
    counts = jax.random.randint(key_count, (NSHARD, NSHARD), 0, PAIR_CAP + 1, dtype=jnp.int32)
    phase = jax.random.randint(key_phase, (), 0, 4, dtype=jnp.int32)
    busy = (shard_ids % 4 == phase)[:, None]
    counts = jnp.where(busy, PAIR_CAP, counts).astype(jnp.int32)
    return (rows, cols, counts)


def draw_pair_row(key, part):
    return pair_tables(key)[0]


def draw_pair_col(key, part):
    return pair_tables(key)[1]


def draw_pair_count(key, part):
    return pair_tables(key)[2]


def draw_qk(key, part):
    key_base = jax.random.fold_in(jax.random.fold_in(key, 11), 0)
    base = jax.random.truncated_normal(key_base, -4.0, 4.0, (TOKENS, H * HD), jnp.float32)
    return base.astype(jnp.bfloat16)


def with_ends(values, rng, least, high):
    extent = values.shape
    place = [jax.random.randint(jax.random.fold_in(rng, axis), (), 0, extent[axis]) for axis in range(len(extent))]
    values = values.at[tuple(place)].set(least)
    longest = extent.index(max(extent))
    place[longest] = (place[longest] + 1) % extent[longest]
    return values.at[tuple(place)].set(high)


def steps_of(key, extent, cuts, least, largest):
    level, own = 1.0, jax.random.fold_in(key, 6)
    for axis_at, blocks in cuts:
        heights = jnp.exp(jax.random.uniform(jax.random.fold_in(own, axis_at), (blocks,), jnp.float32, least / len(cuts), largest / len(cuts)))
        level = level * jnp.repeat(heights, extent[axis_at] // blocks).reshape([-1 if axis == axis_at else 1 for axis in range(len(extent))])
    return level


def normal_values(key, dims, deviation, most, shards=(), kind=jnp.bfloat16):
    result = deviation * jax.random.normal(key, dims, jnp.float32)
    if shards:
        result = result * steps_of(key, dims, shards, -0.22, 0.18)
    return jnp.clip(result, -most, most).astype(kind)


def setup_inputs(seed: int = 0) -> dict:
    key_list = jax.random.split(jax.random.key(seed), 8)
    return {
        "qk": draw_qk(jax.random.fold_in(key_list[7], 71), 0),
        "values": normal_values(key_list[1], (TOKENS, H * HD), 1.0, 6.0, ((0, 8), (1, 4))),
        "bucket": with_ends(jax.random.randint(key_list[2], (NBLK, H), 0, NBUCK), jax.random.fold_in(key_list[2], 1), 0, NBUCK - 1).astype(jnp.int32),
        "pair_row": draw_pair_row(jax.random.fold_in(key_list[7], 71), 0),
        "pair_col": draw_pair_col(jax.random.fold_in(key_list[7], 71), 0),
        "pair_count": draw_pair_count(jax.random.fold_in(key_list[7], 71), 0),
        "w_out": normal_values(key_list[6], (H * HD, D), (H * HD) ** -0.5, 0.125, ((0, 4),)),
    }


NEG = -1e+30

def inverse_norms(block):
    return (lax.rsqrt(lax.optimization_barrier(jnp.mean(block * block, axis=-1)) + 1e-06) / math.sqrt(block.shape[-1])).T

def softmax_side(scores, axis):
    top = lax.optimization_barrier(jnp.max(scores, axis=axis))
    weights = jnp.exp(scores - jnp.expand_dims(top, axis))
    total = lax.optimization_barrier(jnp.sum(weights, axis=axis))
    rounded = lax.optimization_barrier(weights.astype(jnp.bfloat16))
    return (top, total, rounded.astype(jnp.float32))

def pair_parts(q_a, v_a, q_b, v_b, keep):
    f_a = q_a.astype(jnp.float32)
    f_b = q_b.astype(jnp.float32)
    gram = jnp.einsum('shd,thd->hst', f_a, f_b)
    srow = gram * inverse_norms(f_b)[:, None, :]
    scol = gram * inverse_norms(f_a)[:, :, None]
    mrow, lrow, prow = softmax_side(srow, 2)
    acc_row = jnp.einsum('hst,thd->shd', prow, v_b.astype(jnp.float32))
    mcol, lcol, pcol = softmax_side(scol, 1)
    acc_col = jnp.einsum('hst,shd->thd', pcol, v_a.astype(jnp.float32))
    mrow = jnp.where(keep[:, None], mrow, NEG)
    lrow = jnp.where(keep[:, None], lrow, 0.0)
    acc_row = jnp.where(keep[None, :, None], acc_row, 0.0)
    mcol = jnp.where(keep[:, None], mcol, NEG)
    lcol = jnp.where(keep[:, None], lcol, 0.0)
    acc_col = jnp.where(keep[None, :, None], acc_col, 0.0)
    return ((mrow, lrow, acc_row), (mcol, lcol, acc_col))

def diagonal_parts(q_a, v_a):
    f_a = q_a.astype(jnp.float32)
    gram = jnp.einsum('shd,thd->hst', f_a, f_a)
    srow = gram * inverse_norms(f_a)[:, None, :]
    eye = jnp.arange(q_a.shape[0])[:, None] == jnp.arange(q_a.shape[0])[None, :]
    srow = jnp.where(eye[None], NEG, srow)
    mrow, lrow, prow = softmax_side(srow, 2)
    acc_row = jnp.einsum('hst,thd->shd', prow, v_a.astype(jnp.float32))
    return (mrow, lrow, acc_row)

def reference(qk, values, bucket, pair_row, pair_col, pair_count, w_out):
    nsh = pair_row.shape[0]
    cap = pair_row.shape[2]
    q_blocks = qk.reshape(NBLK, BLOCK, H, HD)
    v_blocks = values.reshape(NBLK, BLOCK, H, HD)
    shard_ids = jnp.arange(nsh, dtype=jnp.int32)
    rows_g = (shard_ids[:, None, None] * BPD + pair_row).reshape(-1).astype(jnp.int32)
    cols_g = (shard_ids[None, :, None] * BPD + pair_col).reshape(-1).astype(jnp.int32)
    live = (jnp.arange(cap, dtype=jnp.int32)[None, None, :] < pair_count[:, :, None]).reshape(-1)
    keep = live[:, None] & (bucket[rows_g] == bucket[cols_g])
    groups = rows_g.shape[0] // cap
    xs = (rows_g.reshape(groups, cap), cols_g.reshape(groups, cap), keep.reshape(groups, cap, H))
    diag_m, diag_l, diag_acc = lax.map(lambda a: diagonal_parts(a[0], a[1]), (q_blocks, v_blocks))

    def group_parts(item):
        rg, cg, kp = item
        return jax.vmap(pair_parts)(q_blocks[rg], v_blocks[rg], q_blocks[cg], v_blocks[cg], kp)

    def maxima(item):
        row_side, col_side = group_parts(item)
        return (row_side[0], col_side[0])
    mrow_all, mcol_all = lax.map(maxima, xs)
    m_tot = diag_m.at[rows_g].max(mrow_all.reshape(-1, H, BLOCK))
    m_tot = m_tot.at[cols_g].max(mcol_all.reshape(-1, H, BLOCK))
    scale0 = jnp.exp(diag_m - m_tot)
    l_init = diag_l * scale0
    acc_init = diag_acc * jnp.transpose(scale0, (0, 2, 1))[..., None]

    def accumulate(carry, item):
        l_tot, acc_tot = carry
        rg, cg, kp = item
        row_side, col_side = group_parts(item)
        for idx, side in ((rg, row_side), (cg, col_side)):
            scale = jnp.exp(side[0] - m_tot[idx])
            l_tot = l_tot.at[idx].add(side[1] * scale)
            acc_tot = acc_tot.at[idx].add(side[2] * jnp.transpose(scale, (0, 2, 1))[..., None])
        return ((l_tot, acc_tot), None)
    (l_tot, acc_tot), unused = lax.scan(accumulate, (l_init, acc_init), xs)
    attn = (acc_tot / jnp.transpose(l_tot, (0, 2, 1))[..., None]).reshape(TOKENS, H * HD).astype(jnp.bfloat16)
    return jnp.dot(attn, w_out, preferred_element_type=jnp.float32).astype(jnp.bfloat16)
```

```python
import functools
import math

import jax
import jax.numpy as jnp
from jax import lax
from jax.experimental import pallas as pl
from jax.experimental.pallas import tpu as pltpu
from jax.sharding import PartitionSpec as P

HD = 128
BLOCK = 256
NEG = -1e30
BF16 = jnp.bfloat16
F32 = jnp.float32
SMEM = pl.BlockSpec(memory_space=pltpu.SMEM)
HBM = pl.BlockSpec(memory_space=pl.ANY)


def pack_kernel(q_ref, v_ref, o_ref):
    heads, groups, _, _, rows, _ = o_ref.shape
    for h in range(heads):
        for g in range(groups):
            at = (pl.ds(g * rows, rows), pl.ds(h * HD, HD))
            o_ref[h, g, 0, 0] = q_ref[at]
            o_ref[h, g, 1, 0] = v_ref[at]


def pack(qk, values, spans, groups):
    tokens, width = qk.shape
    heads, span = width // HD, tokens // spans
    rows = span // groups
    block = pl.BlockSpec((span, width), lambda i: (i, 0))
    return pl.pallas_call(
        pack_kernel,
        grid=(spans,),
        in_specs=[block, block],
        out_specs=pl.BlockSpec(
            (heads, groups, 2, 1, rows, HD), lambda i: (0, 0, 0, i, 0, 0)
        ),
        out_shape=jax.ShapeDtypeStruct((heads, groups, 2, spans, rows, HD), BF16),
        cost_estimate=pl.CostEstimate(
            flops=0, bytes_accessed=8 * tokens * width, transcendentals=0
        ),
        name="pack",
    )(qk, values)


def gather_tables(pair_row, pair_col, pair_count, shards):
    mine = jnp.concatenate(
        [pair_row.reshape(-1), pair_col.reshape(-1), pair_count.reshape(-1)]
    )
    have = mine[None]
    me = lax.axis_index("seq")
    step = 1
    while step < shards:
        got = lax.ppermute(have, "seq", [(i, i ^ step) for i in range(shards)])
        low = (me & step) == 0
        have = jnp.concatenate(
            [jnp.where(low, have, got), jnp.where(low, got, have)], axis=0
        )
        step *= 2
    return have.reshape(-1)


def lists_kernel(shards, slots, blocks, cap, tab_ref, bucket_ref, count_ref, list_ref):
    per = shards * slots

    def clear(b, _):
        count_ref[b] = 0
        return 0

    lax.fori_loop(0, shards * blocks, clear, 0)

    def visit(pair, _):
        shard = pair // per
        rest = pair - shard * per
        other = rest // slots
        slot = rest - other * slots
        base = shard * (2 * per + shards)
        a = shard * blocks + tab_ref[base + rest]
        b = other * blocks + tab_ref[base + per + rest]
        live = slot < tab_ref[base + 2 * per + other]

        @pl.when(live & (bucket_ref[a] == bucket_ref[b]))
        def _():
            at = count_ref[a]
            list_ref[a * cap + at] = b
            count_ref[a] = at + 1
            bt = count_ref[b]
            list_ref[b * cap + bt] = a
            count_ref[b] = bt + 1

        return 0

    lax.fori_loop(0, shards * per, visit, 0)


def make_lists(tables, buckets, shards, slots, blocks):
    cap = 2 * shards * slots
    nblk = shards * blocks
    return pl.pallas_call(
        functools.partial(lists_kernel, shards, slots, blocks, cap),
        in_specs=[SMEM, SMEM],
        out_specs=[SMEM, SMEM],
        out_shape=[
            jax.ShapeDtypeStruct((nblk,), jnp.int32),
            jax.ShapeDtypeStruct((nblk * cap,), jnp.int32),
        ],
        name="lists",
    )(tables, buckets)


def attend_kernel(groups, cap, group_ref, count_ref, list_ref, *refs):
    pieces = refs[:groups]
    o_ref, q_ref, v_ref, inv_ref, s_ref, top_ref, sum_ref, acc_ref, sem = refs[groups:]
    units, span, _ = q_ref.shape
    rows = span // groups
    shards, spans = units // pieces[0].shape[2], pieces[0].shape[2]
    blocks_per = span // BLOCK
    me = group_ref[0]

    copies = []
    for r in range(groups):
        piece = lax.rem(me + r, groups)
        for part, ref in enumerate((q_ref, v_ref)):
            for s in range(shards):
                copies.append(
                    pltpu.make_async_copy(
                        pieces[r].at[s, part],
                        ref.at[pl.ds(s * spans, spans), pl.ds(piece * rows, rows), :],
                        sem,
                    )
                )
    for copy in copies:
        copy.start()
    for copy in copies:
        copy.wait()

    def block_at(b):
        unit = b // blocks_per
        return unit, pl.ds(pl.multiple_of((b - unit * blocks_per) * BLOCK, BLOCK), BLOCK)

    ones = jnp.ones((8, HD), BF16)
    contract = (((1,), (1,)), ((), ()))

    def norms(b, _):
        unit, at = block_at(b)
        wide = q_ref[unit, at, :].astype(F32)
        square = wide * wide
        high = square.astype(BF16)
        low = (square - high.astype(F32)).astype(BF16)
        total = lax.dot_general(ones, high, contract, preferred_element_type=F32)
        total += lax.dot_general(ones, low, contract, preferred_element_type=F32)
        scale = math.log2(math.e) / math.sqrt(HD)
        inv_ref[b] = lax.rsqrt(total * (1.0 / HD) + 1e-06) * scale
        return 0

    lax.fori_loop(0, units * blocks_per, norms, 0)

    def unit_body(unit, _):
        query = q_ref[unit, pl.ds(pl.multiple_of(me * rows, rows), rows), :]
        offset = unit * span + me * rows
        own = offset // BLOCK
        n = count_ref[own]

        def scores(b):
            u, at = block_at(b)
            gram = lax.dot_general(
                query, q_ref[u, at, :], contract, preferred_element_type=F32
            )
            return gram * inv_ref[b, 0:1, :]

        shape = (rows, BLOCK)
        diagonal = lax.broadcasted_iota(jnp.int32, shape, 1) == (
            lax.broadcasted_iota(jnp.int32, shape, 0) + (offset - own * BLOCK)
        )
        first = jnp.where(diagonal, NEG, scores(own))
        s_ref[0] = first
        top_ref[...] = jnp.maximum(first[:, :HD], first[:, HD:])

        def score_step(j, _):
            now = scores(list_ref[own * cap + j])
            s_ref[j + 1] = now
            top_ref[...] = jnp.maximum(
                top_ref[...], jnp.maximum(now[:, :HD], now[:, HD:])
            )
            return 0

        lax.fori_loop(0, n, score_step, 0)
        top_ref[...] = jnp.broadcast_to(
            jnp.max(top_ref[...], axis=1, keepdims=True), (rows, HD)
        )

        def weigh(j, b):
            u, at = block_at(b)
            top = top_ref[...]
            left = jnp.exp2(s_ref[j, :, 0:HD] - top)
            right = jnp.exp2(s_ref[j, :, HD : 2 * HD] - top)
            probs = jnp.concatenate([left.astype(BF16), right.astype(BF16)], axis=1)
            return left + right, jnp.dot(
                probs, v_ref[u, at, :], preferred_element_type=F32
            )

        total, acc = weigh(0, own)
        sum_ref[...] = total
        acc_ref[...] = acc

        def weigh_step(j, _):
            total, acc = weigh(j + 1, list_ref[own * cap + j])
            sum_ref[...] += total
            acc_ref[...] += acc
            return 0

        lax.fori_loop(0, n, weigh_step, 0)
        total = jnp.sum(sum_ref[...], axis=1, keepdims=True)
        o_ref[unit] = (acc_ref[...] / total).astype(BF16)
        return 0

    lax.fori_loop(0, units, unit_body, 0)


def attend(group, counts, lists, pieces, cap):
    groups = len(pieces)
    shards, _, spans, rows, _ = pieces[0].shape
    units, span = shards * spans, rows * groups
    nblk = units * span // BLOCK
    jobs = 3 * nblk
    return pl.pallas_call(
        functools.partial(attend_kernel, groups, cap),
        in_specs=[SMEM, SMEM, SMEM] + [HBM] * groups,
        out_specs=pl.BlockSpec(memory_space=pltpu.VMEM),
        out_shape=jax.ShapeDtypeStruct((units, rows, HD), BF16),
        scratch_shapes=[
            pltpu.VMEM((units, span, HD), BF16),
            pltpu.VMEM((units, span, HD), BF16),
            pltpu.VMEM((nblk, 8, BLOCK), F32),
            pltpu.VMEM((cap + 1, rows, BLOCK), F32),
            pltpu.VMEM((rows, HD), F32),
            pltpu.VMEM((rows, HD), F32),
            pltpu.VMEM((rows, HD), F32),
            pltpu.SemaphoreType.DMA,
        ],
        cost_estimate=pl.CostEstimate(
            flops=4 * jobs * rows * BLOCK * HD,
            bytes_accessed=4 * units * span * HD,
            transcendentals=jobs * rows * BLOCK,
        ),
        name="attend",
    )(group, counts, lists, *pieces)


def group_shift(x, shards, groups, r):
    pairs = [
        (i - i % groups + (i % groups + r) % groups, i) for i in range(shards)
    ]
    return lax.ppermute(x, "seq", pairs)


def gather_weights(w_out, shards, groups, member):
    count = lax.axis_size("head")
    here = lax.axis_index("head")
    share = w_out.shape[0] // groups
    take = lambda k: lax.dynamic_slice_in_dim(
        w_out, lax.rem(member + k, groups) * share, share, 0
    )
    mine = take(0)
    ups, downs = {}, {}
    up = down = mine
    for k in range(1, count):
        up = lax.ppermute(up, "head", [(i, i + 1) for i in range(k - 1, count - 1)])
        down = lax.ppermute(down, "head", [(i, i - 1) for i in range(1, count - k + 1)])
        ups[k], downs[k] = up, down
    out = [[take(k) for k in range(groups)]]
    for r in range(1, count):
        piece = jnp.where(here + r < count, downs[r], ups[count - r])
        out.append(
            [piece] + [group_shift(piece, shards, groups, k) for k in range(1, groups)]
        )
    return out


def body(qk, values, bucket, pair_row, pair_col, pair_count, w_out):
    shards = lax.axis_size("seq")
    spans = lax.axis_size("head")
    tokens, width = qk.shape
    heads = width // HD
    groups = shards // heads
    blocks = tokens // BLOCK
    slots = pair_row.shape[2]
    here, z = lax.axis_index("seq"), lax.axis_index("head")
    head, member = here // groups, lax.rem(here, groups)

    sent = pack(qk, values, spans, groups)
    rows = sent.shape[4]
    got = lax.all_to_all(
        sent.reshape(shards, 2, spans, rows, HD), "seq", 0, 0, tiled=True
    )
    pieces = [got] + [group_shift(got, shards, groups, r) for r in range(1, groups)]

    tables = gather_tables(pair_row, pair_col, pair_count, shards)
    buckets = lax.dynamic_slice_in_dim(bucket, z * heads + head, 1, 1).reshape(-1)
    counts, lists = make_lists(tables, buckets, shards, slots, blocks)

    attn = attend(
        member.reshape(1).astype(jnp.int32), counts, lists, pieces, 2 * shards * slots
    )
    weights = gather_weights(w_out, shards, groups, member)

    mixed = lax.all_to_all(attn, ("seq", "head"), 0, 0, tiled=True)
    mixed = mixed.reshape(heads, groups, spans, rows, HD)
    share = w_out.shape[0] // groups
    ordered = jnp.transpose(mixed, (2, 1, 3, 0, 4)).reshape(
        spans, groups * rows, groups, share
    )
    order_z = lax.rem(z + jnp.arange(spans), spans)
    order_g = lax.rem(member + jnp.arange(groups), groups)
    ordered = ordered[order_z][:, :, order_g]
    full = jnp.stack([jnp.stack(pieces_r) for pieces_r in weights])
    summed = jnp.einsum("zrgf,zgfn->rn", ordered, full, preferred_element_type=F32)
    return summed.astype(BF16)


def solution(mesh):
    return jax.shard_map(
        body,
        mesh=mesh,
        in_specs=(
            P("seq", "head"),
            P("seq", "head"),
            P(),
            P("seq", None, None),
            P("seq", None, None),
            P("seq", None),
            P("head", None),
        ),
        out_specs=P(("seq", "head"), None),
        check_vma=False,
    )
```

```python
import functools
import math

import jax
import jax.numpy as jnp
from jax import lax
from jax.experimental import pallas as pl
from jax.experimental.pallas import tpu as pltpu
from jax.sharding import PartitionSpec as P


HD = 128
BLOCK = 256
NEG = -1e30
LEAD, TAIL = 2, 6
PREP_STEP = 4
BF16 = jnp.bfloat16
F32 = jnp.float32
SMEM = pl.BlockSpec(memory_space=pltpu.SMEM)
HBM = pl.BlockSpec(memory_space=pl.ANY)


def pack_kernel(q_ref, v_ref, o_ref):
    heads, groups, _, _, rows, _ = o_ref.shape
    for h in range(heads):
        for g in range(groups):
            at = (pl.ds(g * rows, rows), pl.ds(h * HD, HD))
            o_ref[h, g, 0, 0] = q_ref[at]
            o_ref[h, g, 1, 0] = v_ref[at]


def pack(qk, values, spans, groups):
    tokens, width = qk.shape
    heads, span = width // HD, tokens // spans
    rows = span // groups
    block = pl.BlockSpec((span, width), lambda i: (i, 0))
    return pl.pallas_call(
        pack_kernel,
        grid=(spans,),
        in_specs=[block, block],
        out_specs=pl.BlockSpec(
            (heads, groups, 2, 1, rows, HD), lambda i: (0, 0, 0, i, 0, 0)
        ),
        out_shape=jax.ShapeDtypeStruct((heads, groups, 2, spans, rows, HD), BF16),
        cost_estimate=pl.CostEstimate(
            flops=0, bytes_accessed=8 * tokens * width, transcendentals=0
        ),
        name="pack",
    )(qk, values)


def gather_tables(pair_row, pair_col, pair_count, shards):
    mine = jnp.concatenate(
        [pair_row.reshape(-1), pair_col.reshape(-1), pair_count.reshape(-1)]
    )
    rest = [
        lax.ppermute(mine, "seq", [((i + r) % shards, i) for i in range(shards)])
        for r in range(1, shards)
    ]
    return jnp.concatenate([mine] + rest)


def job_lists(tables, buckets, spot, shards, slots, blocks, units, span, rows):
    nblk = shards * blocks
    cap = 2 * shards * slots
    limit = job_limit(units, shards, slots)

    def kernel(tab_ref, bucket_ref, spot_ref, count_ref, unit_ref, key_ref, fill, lists):
        def clear(b, _):
            fill[b] = 0
            return 0

        lax.fori_loop(0, nblk, clear, 0)
        per = shards * slots

        def visit(pair, _):
            shard = pair // per
            rest = pair - shard * per
            other = rest // slots
            slot = rest - other * slots
            base = lax.rem(shard + shards - spot_ref[2], shards) * (2 * per + shards)
            a = shard * blocks + tab_ref[base + rest]
            b = other * blocks + tab_ref[base + per + rest]
            live = slot < tab_ref[base + 2 * per + other]

            @pl.when(live & (bucket_ref[a] == bucket_ref[b]))
            def _():
                at = fill[a]
                lists[a * cap + at] = b
                fill[a] = at + 1
                bt = fill[b]
                lists[b * cap + bt] = a
                fill[b] = bt + 1

            return 0

        lax.fori_loop(0, shards * per, visit, 0)

        for i in range(LEAD):
            unit_ref[i] = units
            key_ref[i] = 0

        def per_unit(unit, at):
            own = (unit * span + spot_ref[0] * rows) // BLOCK
            unit_ref[at] = unit
            key_ref[at] = own
            n = fill[own]

            def partner(j, _):
                unit_ref[at + 1 + j] = unit
                key_ref[at + 1 + j] = lists[own * cap + j]
                return 0

            lax.fori_loop(0, n, partner, 0)
            return at + 1 + n

        end = lax.fori_loop(0, units, per_unit, LEAD)
        for i in range(TAIL):
            unit_ref[end + i] = units
            key_ref[end + i] = 0
        count_ref[0] = end - LEAD

    return pl.pallas_call(
        kernel,
        in_specs=[SMEM, SMEM, SMEM],
        out_specs=[SMEM, SMEM, SMEM],
        out_shape=[
            jax.ShapeDtypeStruct((1,), jnp.int32),
            jax.ShapeDtypeStruct((limit,), jnp.int32),
            jax.ShapeDtypeStruct((limit,), jnp.int32),
        ],
        scratch_shapes=[
            pltpu.SMEM((nblk,), jnp.int32),
            pltpu.SMEM((nblk * cap,), jnp.int32),
        ],
        cost_estimate=pl.CostEstimate(
            flops=0, bytes_accessed=32 * 1024 * 1024, transcendentals=0
        ),
        name="job_lists",
    )(tables, buckets, spot)


def job_limit(units, shards, slots):
    return units + 2 * shards * shards * slots + LEAD + TAIL


def attend_kernel(groups, spot_ref, count_ref, unit_ref, key_ref, *refs):
    pieces = refs[:groups]
    o_ref, q_ref, v_ref, vt_ref, inv_ref, s0, s1, x0, x1, p0, p1, a0, a1 = refs[
        groups : groups + 13
    ]
    top_ref, sum_ref, acc_ref, q_sem, v_sem = refs[groups + 13 :]
    units, span, _ = q_ref.shape
    rows = span // groups
    spans = pieces[0].shape[2]
    shards = units // spans
    blocks_per = span // BLOCK
    me = spot_ref[0]
    lanes = [slice(k, min(k + HD, rows)) for k in range(0, rows, HD)]

    copies = ([], [])
    for r in range(groups):
        piece = lax.rem(me + r, groups)
        for part, ref, sem in ((0, q_ref, q_sem), (1, v_ref, v_sem)):
            for s in range(shards):
                copies[part].append(
                    pltpu.make_async_copy(
                        pieces[r].at[s, part],
                        ref.at[pl.ds(s * spans, spans), pl.ds(piece * rows, rows), :],
                        sem,
                    )
                )
    for part in copies:
        for copy in part:
            copy.start()

    def clear(unit, _):
        sum_ref[unit] = jnp.zeros(sum_ref.shape[1:], F32)
        acc_ref[unit] = jnp.zeros(acc_ref.shape[1:], F32)
        return 0

    lax.fori_loop(0, units + 1, clear, 0)
    for part in copies:
        for copy in part:
            copy.wait()

    def block_at(b):
        if blocks_per == 1:
            return b, slice(None)
        unit = b // blocks_per
        return unit, pl.ds(pl.multiple_of((b - unit * blocks_per) * BLOCK, BLOCK), BLOCK)

    ones = jnp.ones((HD, HD), BF16)
    contract = (((1,), (1,)), ((), ()))

    def prepare(i, _):
        for k in range(PREP_STEP):
            b = i * PREP_STEP + k
            unit, at = block_at(b)
            wide = q_ref[unit, at, :].astype(F32)
            square = wide * wide
            high = square.astype(BF16)
            low = (square - high.astype(F32)).astype(BF16)
            total = jnp.dot(high, ones, preferred_element_type=F32)
            total += jnp.dot(low, ones, preferred_element_type=F32)
            scale = math.log2(math.e) / math.sqrt(HD)
            inv_ref[b] = lax.rsqrt(total * (1.0 / HD) + 1e-06) * scale
            vt_ref[b] = v_ref[unit, at, :].T
        return 0

    lax.fori_loop(0, units * blocks_per // PREP_STEP, prepare, 0)

    def tiles(x):
        return x.reshape(x.shape[0] // 8, 8, x.shape[1])

    def score(t, s_ref, x_ref):
        unit, key = jnp.minimum(unit_ref[t], units - 1), key_ref[t]
        first = unit_ref[t - 1] != unit_ref[t]
        query = q_ref[unit, pl.ds(pl.multiple_of(me * rows, rows), rows), :]
        u, at = block_at(key)
        gram = lax.dot_general(q_ref[u, at, :], query, contract, preferred_element_type=F32)
        offset = lax.rem(unit * span + me * rows, BLOCK)
        shift = jnp.where(first, offset, 2 * BLOCK)
        for lane in lanes:
            n = lane.stop - lane.start
            part = gram[:, lane] * inv_ref[key, :, 0:n]
            lo, hi = (lane.start, lane.stop) if rows == BLOCK else (0, BLOCK)
            band = part[lo:hi]
            row = lax.broadcasted_iota(jnp.int32, band.shape, 0) + (lo - lane.start)
            col = lax.broadcasted_iota(jnp.int32, band.shape, 1)
            band = jnp.where(row - col == shift, NEG, band)
            above = [part[:lo]] if lo else []
            below = [part[hi:]] if hi < BLOCK else []
            part = jnp.concatenate(above + [band] + below, axis=0)
            s_ref[:, lane] = part
            most = jnp.max(jnp.max(tiles(part), axis=0), axis=0, keepdims=True)
            x_ref[:, lane] = jnp.broadcast_to(most, (8, n))

    def weigh(t, s_ref, x_ref, p_ref, a_ref):
        unit = unit_ref[t]
        first = unit_ref[t - 1] != unit
        old = jnp.where(first, 2 * NEG, top_ref[...])
        new = jnp.maximum(old, x_ref[...])
        top_ref[...] = new
        scale = jnp.exp2(old - new)
        a_ref[...] = scale
        for lane in lanes:
            prob = jnp.exp2(tiles(s_ref[:, lane]) - new[None, :, lane])
            sum_ref[unit, :, lane] = sum_ref[unit, :, lane] * scale[:, lane] + jnp.sum(
                prob, axis=0
            )
            p_ref[:, lane] = prob.reshape(BLOCK, lane.stop - lane.start).astype(BF16)

    def gather(t, p_ref, a_ref):
        unit, key = unit_ref[t], key_ref[t]
        part = jnp.dot(vt_ref[key], p_ref[...], preferred_element_type=F32)
        kept = tiles(acc_ref[unit]) * a_ref[...][None]
        acc_ref[unit] = kept.reshape(HD, rows) + part

    def pair_step(i, _):
        t = LEAD + 2 * i
        gather(t - 2, p0, a0)
        weigh(t - 1, s1, x1, p1, a1)
        score(t, s0, x0)
        gather(t - 1, p1, a1)
        weigh(t, s0, x0, p0, a0)
        score(t + 1, s1, x1)
        return 0

    lax.fori_loop(0, (count_ref[0] + 1) // 2 + 1, pair_step, 0)

    def finish(unit, _):
        total = 1.0 / jnp.sum(sum_ref[unit], axis=0, keepdims=True)
        o_ref[unit] = (acc_ref[unit] * total).T.astype(BF16)
        return 0

    lax.fori_loop(0, units, finish, 0)


def attend(spot, jobs, pieces):
    groups = len(pieces)
    shards, _, spans, rows, _ = pieces[0].shape
    units, span = shards * spans, rows * groups
    nblk = units * span // BLOCK
    work = 3 * units
    scores = pltpu.VMEM((BLOCK, rows), F32)
    probs = pltpu.VMEM((BLOCK, rows), BF16)
    line = pltpu.VMEM((8, rows), F32)
    return pl.pallas_call(
        functools.partial(attend_kernel, groups),
        in_specs=[SMEM] * 4 + [HBM] * groups,
        out_specs=pl.BlockSpec(memory_space=pltpu.VMEM),
        out_shape=jax.ShapeDtypeStruct((units, rows, HD), BF16),
        scratch_shapes=[
            pltpu.VMEM((units, span, HD), BF16),
            pltpu.VMEM((units, span, HD), BF16),
            pltpu.VMEM((nblk, HD, BLOCK), BF16),
            pltpu.VMEM((nblk, BLOCK, HD), F32),
            *[scores, scores, line, line, probs, probs, line, line],
            line,
            pltpu.VMEM((units + 1, 8, rows), F32),
            pltpu.VMEM((units + 1, HD, rows), F32),
            pltpu.SemaphoreType.DMA,
            pltpu.SemaphoreType.DMA,
        ],
        cost_estimate=pl.CostEstimate(
            flops=4 * work * rows * BLOCK * HD,
            bytes_accessed=4 * units * span * HD,
            transcendentals=work * rows * BLOCK,
        ),
        name="attend",
    )(spot, *jobs, *pieces)


def group_shift(x, shards, groups, r):
    pairs = [(i - i % groups + (i % groups + r) % groups, i) for i in range(shards)]
    return lax.ppermute(x, "seq", pairs)


def gather_weights(w_out, groups, member):
    count = lax.axis_size("head")
    share = w_out.shape[0] // groups
    mine = lax.dynamic_slice_in_dim(w_out, member * share, share, 0)
    return [
        lax.ppermute(mine, "head", [((i + r) % count, i) for i in range(count)])
        for r in range(1, count)
    ]


def project_kernel(spot_ref, x_ref, w_ref, *refs):
    heads, groups, spans, rows, _ = x_ref.shape
    pieces = refs[: (spans - 1) * groups]
    o_ref, wide_ref, w_buf, sem = refs[(spans - 1) * groups :]
    member, z = spot_ref[0], spot_ref[1]
    tile = w_buf.shape[2]
    share = pieces[0].shape[0]
    depth = heads * HD
    step, steps = pl.program_id(0), pl.num_programs(0)

    def copies(i):
        slot = lax.rem(i, 2)
        cols = pl.ds(pl.multiple_of(i * tile, tile), tile)
        out = [
            pltpu.make_async_copy(
                w_ref.at[:, cols],
                w_buf.at[slot, pl.ds(pl.multiple_of(z * depth, depth), depth), :],
                sem.at[slot],
            )
        ]
        for r in range(1, spans):
            for k in range(groups):
                at = lax.rem(z + r, spans) * depth + lax.rem(member + k, groups) * share
                out.append(
                    pltpu.make_async_copy(
                        pieces[(r - 1) * groups + k].at[:, cols],
                        w_buf.at[slot, pl.ds(pl.multiple_of(at, share), share), :],
                        sem.at[slot],
                    )
                )
        return out

    @pl.when(step == 0)
    def _():
        for copy in copies(step):
            copy.start()
        for z_at in range(spans):
            for h in range(heads):
                at = (z_at * heads + h) * HD
                for g in range(groups):
                    wide_ref[g * rows : (g + 1) * rows, at : at + HD] = x_ref[h, g, z_at]

    @pl.when(step + 1 < steps)
    def _():
        for copy in copies(step + 1):
            copy.start()

    for copy in copies(step):
        copy.wait()
    o_ref[...] = jnp.dot(
        wide_ref[...], w_buf[lax.rem(step, 2)], preferred_element_type=F32
    ).astype(BF16)


def project(spot, mixed, w_out, pieces):
    _, groups, spans, rows, _ = mixed.shape
    depth, width = w_out.shape
    tile = min(512, width)
    out_rows = groups * rows
    return pl.pallas_call(
        project_kernel,
        grid=(width // tile,),
        in_specs=[SMEM, pl.BlockSpec(memory_space=pltpu.VMEM)] + [HBM] * (1 + len(pieces)),
        out_specs=pl.BlockSpec((out_rows, tile), lambda i: (0, i)),
        out_shape=jax.ShapeDtypeStruct((out_rows, width), BF16),
        scratch_shapes=[
            pltpu.VMEM((out_rows, spans * depth), BF16),
            pltpu.VMEM((2, spans * depth, tile), BF16),
            pltpu.SemaphoreType.DMA((2,)),
        ],
        cost_estimate=pl.CostEstimate(
            flops=2 * out_rows * spans * depth * width,
            bytes_accessed=2 * spans * depth * width,
            transcendentals=0,
        ),
        name="project",
    )(spot, mixed, w_out, *pieces)


def body(qk, values, bucket, pair_row, pair_col, pair_count, w_out):
    shards = lax.axis_size("seq")
    spans = lax.axis_size("head")
    tokens, width = qk.shape
    heads = width // HD
    groups = shards // heads
    blocks = tokens // BLOCK
    slots = pair_row.shape[2]
    here, z = lax.axis_index("seq"), lax.axis_index("head")
    head, member = here // groups, lax.rem(here, groups)
    spot = jnp.stack([member, z, here]).astype(jnp.int32)

    shares = gather_weights(w_out, groups, member)
    sent = pack(qk, values, spans, groups)
    rows = sent.shape[4]
    got = lax.all_to_all(
        sent.reshape(shards, 2, spans, rows, HD), "seq", 0, 0, tiled=True
    )
    pieces = [got] + [group_shift(got, shards, groups, r) for r in range(1, groups)]

    tables = gather_tables(pair_row, pair_col, pair_count, shards)
    buckets = lax.dynamic_slice_in_dim(bucket, z * heads + head, 1, 1).reshape(-1)
    units = shards * spans
    jobs = job_lists(
        tables, buckets, spot, shards, slots, blocks, units, tokens // spans, rows
    )
    attn = attend(spot, jobs, pieces)
    mixed = lax.all_to_all(attn, ("seq", "head"), 0, 0, tiled=True)
    mixed = mixed.reshape(heads, groups, spans, rows, HD)
    weights = []
    for piece in shares:
        weights += [piece] + [
            group_shift(piece, shards, groups, k) for k in range(1, groups)
        ]
    return project(spot, mixed, w_out, weights)


def solution(mesh):
    return jax.shard_map(
        body,
        mesh=mesh,
        in_specs=(
            P("seq", "head"),
            P("seq", "head"),
            P(),
            P("seq", None, None),
            P("seq", None, None),
            P("seq", None),
            P("head", None),
        ),
        out_specs=P(("seq", "head"), None),
        check_vma=False,
    )
```

```python
import functools
import math

import jax
import jax.numpy as jnp
from jax import lax
from jax.experimental import pallas as pl
from jax.experimental.pallas import tpu as pltpu
from jax.sharding import PartitionSpec as P


HD = 128
BLOCK = 256
NEG = -1e30
LEAD, TAIL = 2, 14
PREP_STEP = 4
CHUNK = 8
VALUE_STEP = 4
FINISH_STEP = 4
BF16 = jnp.bfloat16
F32 = jnp.float32
SMEM = pl.BlockSpec(memory_space=pltpu.SMEM)
HBM = pl.BlockSpec(memory_space=pl.ANY)


def pack_kernel(turned, x_ref, o_ref):
    heads, groups = o_ref.shape[:2]
    rows = x_ref.shape[0] // groups
    for h in range(heads):
        for g in range(groups):
            part = x_ref[g * rows : (g + 1) * rows, h * HD : (h + 1) * HD]
            o_ref[h, g, 0] = part.T if turned else part


def pack(x, spans, groups, turned=False):
    tokens, width = x.shape
    heads, span = width // HD, tokens // spans
    rows = span // groups
    tail = (HD, rows) if turned else (rows, HD)
    return pl.pallas_call(
        functools.partial(pack_kernel, turned),
        grid=(spans,),
        in_specs=[pl.BlockSpec((span, width), lambda i: (i, 0))],
        out_specs=pl.BlockSpec((heads, groups, 1, *tail), lambda i: (0, 0, i, 0, 0)),
        out_shape=jax.ShapeDtypeStruct((heads, groups, spans, *tail), BF16),
        cost_estimate=pl.CostEstimate(
            flops=0, bytes_accessed=4 * tokens * width, transcendentals=0
        ),
        name="pack",
    )(x)


def gather_tables(pair_row, pair_col, pair_count, shards):
    mine = jnp.concatenate(
        [pair_row.reshape(-1), pair_col.reshape(-1), pair_count.reshape(-1)]
    )
    rest = [
        lax.ppermute(mine, "seq", [((i + r) % shards, i) for i in range(shards)])
        for r in range(1, shards)
    ]
    return jnp.concatenate([mine] + rest)


def job_lists(tables, buckets, spot, shards, slots, blocks, units, span, rows):
    nblk = shards * blocks
    cap = 2 * shards * slots
    limit = job_limit(units, shards, slots)

    def kernel(tab_ref, bucket_ref, spot_ref, count_ref, unit_ref, key_ref, fill, lists):
        def clear(b, _):
            fill[b] = 0
            return 0

        lax.fori_loop(0, nblk, clear, 0)
        per = shards * slots

        def visit(pair, _):
            shard = pair // per
            rest = pair - shard * per
            other = rest // slots
            slot = rest - other * slots
            base = lax.rem(shard + shards - spot_ref[2], shards) * (2 * per + shards)
            a = shard * blocks + tab_ref[base + rest]
            b = other * blocks + tab_ref[base + per + rest]
            live = slot < tab_ref[base + 2 * per + other]

            @pl.when(live & (bucket_ref[a] == bucket_ref[b]))
            def _():
                at = fill[a]
                lists[a * cap + at] = b
                fill[a] = at + 1
                bt = fill[b]
                lists[b * cap + bt] = a
                fill[b] = bt + 1

            return 0

        lax.fori_loop(0, shards * per, visit, 0)

        for i in range(LEAD):
            unit_ref[i] = units
            key_ref[i] = 0

        def per_unit(unit, at):
            own = (unit * span + spot_ref[0] * rows) // BLOCK
            unit_ref[at] = unit
            key_ref[at] = own
            n = fill[own]

            def partner(j, _):
                unit_ref[at + 1 + j] = unit
                key_ref[at + 1 + j] = lists[own * cap + j]
                return 0

            lax.fori_loop(0, n, partner, 0)
            return at + 1 + n

        end = lax.fori_loop(0, units, per_unit, LEAD)
        for i in range(TAIL):
            unit_ref[end + i] = units
            key_ref[end + i] = 0
        count_ref[0] = end - LEAD

    return pl.pallas_call(
        kernel,
        in_specs=[SMEM, SMEM, SMEM],
        out_specs=[SMEM, SMEM, SMEM],
        out_shape=[
            jax.ShapeDtypeStruct((1,), jnp.int32),
            jax.ShapeDtypeStruct((limit,), jnp.int32),
            jax.ShapeDtypeStruct((limit,), jnp.int32),
        ],
        scratch_shapes=[
            pltpu.SMEM((nblk,), jnp.int32),
            pltpu.SMEM((nblk * cap,), jnp.int32),
        ],
        cost_estimate=pl.CostEstimate(
            flops=0, bytes_accessed=32 * 1024 * 1024, transcendentals=0
        ),
        name="job_lists",
    )(tables, buckets, spot)


def job_limit(units, shards, slots):
    return units + 2 * shards * shards * slots + LEAD + TAIL


def attend_kernel(groups, spot_ref, count_ref, unit_ref, key_ref, *refs):
    pieces = refs[:groups], refs[groups : 2 * groups]
    refs = refs[groups:]
    o_ref, q_ref, v_ref, vt_ref, inv_ref, s0, s1, x0, x1, p0, p1, a0, a1 = refs[
        groups : groups + 13
    ]
    top_ref, sum_ref, acc_ref, q_sem, v_sem = refs[groups + 13 :]
    units, span, _ = q_ref.shape
    rows = span // groups
    spans = pieces[0][0].shape[1]
    shards = units // spans
    blocks_per = span // BLOCK
    me = spot_ref[0]
    lanes = [slice(k, min(k + HD, rows)) for k in range(0, rows, HD)]

    copies = ([], [])
    for r in range(groups):
        piece = lax.rem(me + r, groups)
        for part, ref, sem in ((0, q_ref, q_sem), (1, v_ref, v_sem)):
            for s in range(shards):
                copies[part].append(
                    pltpu.make_async_copy(
                        pieces[part][r].at[s],
                        ref.at[pl.ds(s * spans, spans), pl.ds(piece * rows, rows), :],
                        sem,
                    )
                )
    for part in copies:
        for copy in part:
            copy.start()

    def clear(unit, _):
        sum_ref[unit] = jnp.zeros(sum_ref.shape[1:], F32)
        acc_ref[unit] = jnp.zeros(acc_ref.shape[1:], F32)
        return 0

    lax.fori_loop(0, units + 1, clear, 0)
    for part in copies:
        for copy in part:
            copy.wait()

    def block_at(b):
        if blocks_per == 1:
            return b, slice(None)
        unit = b // blocks_per
        return unit, pl.ds(pl.multiple_of((b - unit * blocks_per) * BLOCK, BLOCK), BLOCK)

    ones = jnp.ones((HD, HD), BF16)
    contract = (((1,), (1,)), ((), ()))

    def prepare(i, _):
        for k in range(PREP_STEP):
            b = i * PREP_STEP + k
            unit, at = block_at(b)
            wide = q_ref[unit, at, :].astype(F32)
            square = wide * wide
            high = square.astype(BF16)
            low = (square - high.astype(F32)).astype(BF16)
            total = jnp.dot(high, ones, preferred_element_type=F32)
            total += jnp.dot(low, ones, preferred_element_type=F32)
            scale = math.log2(math.e) / math.sqrt(HD)
            inv_ref[b] = lax.rsqrt(total * (1.0 / HD) + 1e-06) * scale
            vt_ref[b] = v_ref[unit, at, :].T
        return 0

    lax.fori_loop(0, units * blocks_per // PREP_STEP, prepare, 0)

    def tiles(x):
        return x.reshape(x.shape[0] // 8, 8, x.shape[1])

    def score(t, s_ref, x_ref):
        unit, key = jnp.minimum(unit_ref[t], units - 1), key_ref[t]
        first = unit_ref[t - 1] != unit_ref[t]
        query = q_ref[unit, pl.ds(pl.multiple_of(me * rows, rows), rows), :]
        u, at = block_at(key)
        gram = lax.dot_general(q_ref[u, at, :], query, contract, preferred_element_type=F32)
        offset = lax.rem(unit * span + me * rows, BLOCK)
        shift = jnp.where(first, offset, 2 * BLOCK)
        for lane in lanes:
            n = lane.stop - lane.start
            part = gram[:, lane] * inv_ref[key, :, 0:n]
            lo, hi = (lane.start, lane.stop) if rows == BLOCK else (0, BLOCK)
            band = part[lo:hi]
            row = lax.broadcasted_iota(jnp.int32, band.shape, 0) + (lo - lane.start)
            col = lax.broadcasted_iota(jnp.int32, band.shape, 1)
            band = jnp.where(row - col == shift, NEG, band)
            above = [part[:lo]] if lo else []
            below = [part[hi:]] if hi < BLOCK else []
            part = jnp.concatenate(above + [band] + below, axis=0)
            s_ref[:, lane] = part
            most = jnp.max(jnp.max(tiles(part), axis=0), axis=0, keepdims=True)
            x_ref[:, lane] = jnp.broadcast_to(most, (8, n))

    def weigh(t, s_ref, x_ref, p_ref, a_ref):
        unit = unit_ref[t]
        first = unit_ref[t - 1] != unit
        old = jnp.where(first, 2 * NEG, top_ref[...])
        new = jnp.maximum(old, x_ref[...])
        top_ref[...] = new
        scale = jnp.exp2(old - new)
        a_ref[...] = scale
        for lane in lanes:
            prob = jnp.exp2(tiles(s_ref[:, lane]) - new[None, :, lane])
            sum_ref[unit, :, lane] = sum_ref[unit, :, lane] * scale[:, lane] + jnp.sum(
                prob, axis=0
            )
            p_ref[:, lane] = prob.reshape(BLOCK, lane.stop - lane.start).astype(BF16)

    def gather(t, p_ref, a_ref):
        unit, key = unit_ref[t], key_ref[t]
        part = jnp.dot(vt_ref[key], p_ref[...], preferred_element_type=F32)
        kept = tiles(acc_ref[unit]) * a_ref[...][None]
        acc_ref[unit] = kept.reshape(HD, rows) + part

    def pair_step(i, _):
        t = LEAD + 2 * i
        gather(t - 2, p0, a0)
        weigh(t - 1, s1, x1, p1, a1)
        score(t, s0, x0)
        gather(t - 1, p1, a1)
        weigh(t, s0, x0, p0, a0)
        score(t + 1, s1, x1)
        return 0

    lax.fori_loop(0, (count_ref[0] + 1) // 2 + 1, pair_step, 0)

    def finish(unit, _):
        total = 1.0 / jnp.sum(sum_ref[unit], axis=0, keepdims=True)
        o_ref[unit] = (acc_ref[unit] * total).T.astype(BF16)
        return 0

    lax.fori_loop(0, units, finish, 0)


def attend(spot, jobs, q_pieces, v_pieces):
    groups = len(q_pieces)
    shards, spans, rows, _ = q_pieces[0].shape
    units, span = shards * spans, rows * groups
    nblk = units * span // BLOCK
    work = 3 * units
    scores = pltpu.VMEM((BLOCK, rows), F32)
    probs = pltpu.VMEM((BLOCK, rows), BF16)
    line = pltpu.VMEM((8, rows), F32)
    return pl.pallas_call(
        functools.partial(attend_kernel, groups),
        in_specs=[SMEM] * 4 + [HBM] * (2 * groups),
        out_specs=pl.BlockSpec(memory_space=pltpu.VMEM),
        out_shape=jax.ShapeDtypeStruct((units, rows, HD), BF16),
        scratch_shapes=[
            pltpu.VMEM((units, span, HD), BF16),
            pltpu.VMEM((units, span, HD), BF16),
            pltpu.VMEM((nblk, HD, BLOCK), BF16),
            pltpu.VMEM((nblk, BLOCK, HD), F32),
            *[scores, scores, line, line, probs, probs, line, line],
            line,
            pltpu.VMEM((units + 1, 8, rows), F32),
            pltpu.VMEM((units + 1, HD, rows), F32),
            pltpu.SemaphoreType.DMA,
            pltpu.SemaphoreType.DMA,
        ],
        cost_estimate=pl.CostEstimate(
            flops=4 * work * rows * BLOCK * HD,
            bytes_accessed=4 * units * span * HD,
            transcendentals=work * rows * BLOCK,
        ),
        name="attend",
    )(spot, *jobs, *q_pieces, *v_pieces)


def scores_kernel(groups, spot_ref, count_ref, unit_ref, key_ref, *refs):
    pieces = refs[:groups]
    p_out, scale_ref, sum_ref, q_ref, inv_ref, s0, s1, x0, x1, top_ref, p_buf, q_sem, p_sem = refs[
        groups:
    ]
    shards, spans, rows, _ = pieces[0].shape
    units = shards * spans
    me = spot_ref[0]
    lanes = [slice(k, k + HD) for k in range(0, rows, HD)]

    copies = []
    for r in range(groups):
        piece = lax.rem(me + r, groups)
        for s in range(shards):
            copies.append(
                pltpu.make_async_copy(
                    pieces[r].at[s], q_ref.at[pl.ds(s * spans, spans), piece], q_sem
                )
            )
    for copy in copies:
        copy.start()
    sum_ref[...] = jnp.zeros(sum_ref.shape, F32)
    for copy in copies:
        copy.wait()

    ones = jnp.ones((HD, HD), BF16)
    contract = (((1,), (1,)), ((), ()))

    def prepare(i, _):
        for k in range(PREP_STEP):
            b = i * PREP_STEP + k
            wide = q_ref[b // groups, lax.rem(b, groups)].astype(F32)
            square = wide * wide
            high = square.astype(BF16)
            low = (square - high.astype(F32)).astype(BF16)
            total = jnp.dot(high, ones, preferred_element_type=F32)
            total += jnp.dot(low, ones, preferred_element_type=F32)
            scale = math.log2(math.e) / math.sqrt(HD)
            inv_ref[b] = lax.rsqrt(total * (1.0 / HD) + 1e-06) * scale
        return 0

    lax.fori_loop(0, units * groups // PREP_STEP, prepare, 0)

    def tiles(x):
        return x.reshape(x.shape[0] // 8, 8, x.shape[1])

    def score(j, s_ref, x_ref):
        t = LEAD + j
        unit, key = jnp.minimum(unit_ref[t], units - 1), key_ref[t]
        first = unit_ref[t - 1] != unit_ref[t]
        gram = lax.dot_general(
            q_ref[key // groups, lax.rem(key, groups)],
            q_ref[unit, me],
            contract,
            preferred_element_type=F32,
        )
        shift = jnp.where(first, 0, 2 * BLOCK)
        for lane in lanes:
            part = gram[:, lane] * inv_ref[key]
            band = part[lane]
            row = lax.broadcasted_iota(jnp.int32, band.shape, 0)
            col = lax.broadcasted_iota(jnp.int32, band.shape, 1)
            band = jnp.where(row - col == shift, NEG, band)
            above = [part[: lane.start]] if lane.start else []
            below = [part[lane.stop :]] if lane.stop < BLOCK else []
            part = jnp.concatenate(above + [band] + below, axis=0)
            s_ref[:, lane] = part
            most = jnp.max(jnp.max(tiles(part), axis=0), axis=0, keepdims=True)
            x_ref[:, lane] = jnp.broadcast_to(most, (8, HD))

    def weigh(j, s_ref, x_ref, slot, at):
        unit = unit_ref[LEAD + j]
        first = unit_ref[LEAD + j - 1] != unit
        old = jnp.where(first, 2 * NEG, top_ref[...])
        new = jnp.maximum(old, x_ref[...])
        top_ref[...] = new
        scale = jnp.exp2(old - new)
        scale_ref[pl.ds(j, 1), :] = scale[0:1]
        total = sum_ref[unit] * scale
        for lane in lanes:
            prob = jnp.exp2(tiles(s_ref[:, lane]) - new[None, :, lane])
            sum_ref[unit, :, lane] = total[:, lane] + jnp.sum(prob, axis=0)
            p_buf[slot, at, :, lane] = prob.reshape(BLOCK, HD).astype(BF16)

    def out_copy(chunk):
        slot = lax.rem(chunk, 2)
        return pltpu.make_async_copy(
            p_buf.at[slot], p_out.at[pl.ds(chunk * CHUNK, CHUNK)], p_sem.at[slot]
        )

    score(0, s0, x0)
    score(1, s1, x1)
    chunks = (count_ref[0] + CHUNK - 1) // CHUNK

    def chunk_step(chunk, _):
        slot = lax.rem(chunk, 2)

        @pl.when(chunk >= 2)
        def _():
            out_copy(chunk - 2).wait()

        def step(k, _):
            j = chunk * CHUNK + 2 * k
            weigh(j, s0, x0, slot, 2 * k)
            weigh(j + 1, s1, x1, slot, 2 * k + 1)
            score(j + 2, s0, x0)
            score(j + 3, s1, x1)
            return 0

        lax.fori_loop(0, CHUNK // 2, step, 0)
        out_copy(chunk).start()
        return 0

    lax.fori_loop(0, chunks, chunk_step, 0)
    for back in (2, 1):

        @pl.when(chunks >= back)
        def _():
            out_copy(chunks - back).wait()


def attend_scores(spot, jobs, pieces):
    groups = len(pieces)
    shards, spans, rows, _ = pieces[0].shape
    units = shards * spans
    nblk = units * groups
    room = jobs[1].shape[0] // CHUNK * CHUNK
    work = 3 * units
    vmem = pl.BlockSpec(memory_space=pltpu.VMEM)
    return pl.pallas_call(
        functools.partial(scores_kernel, groups),
        in_specs=[SMEM] * 4 + [HBM] * groups,
        out_specs=[HBM, vmem, vmem],
        out_shape=[
            jax.ShapeDtypeStruct((room, BLOCK, rows), BF16),
            jax.ShapeDtypeStruct((room, rows), F32),
            jax.ShapeDtypeStruct((units + 1, 8, rows), F32),
        ],
        scratch_shapes=[
            pltpu.VMEM((units, groups, rows, HD), BF16),
            pltpu.VMEM((nblk, BLOCK, HD), F32),
            pltpu.VMEM((BLOCK, rows), F32),
            pltpu.VMEM((BLOCK, rows), F32),
            *[pltpu.VMEM((8, rows), F32)] * 3,
            pltpu.VMEM((2, CHUNK, BLOCK, rows), BF16),
            pltpu.SemaphoreType.DMA,
            pltpu.SemaphoreType.DMA((2,)),
        ],
        cost_estimate=pl.CostEstimate(
            flops=2 * work * rows * BLOCK * HD,
            bytes_accessed=2 * units * groups * rows * HD + 2 * work * rows * BLOCK,
            transcendentals=work * rows * BLOCK,
        ),
        name="attend_scores",
    )(spot, *jobs, *pieces)


def values_kernel(groups, spot_ref, count_ref, unit_ref, key_ref, *refs):
    pieces = refs[:groups]
    p_in, scale_ref, sum_ref, o_ref, vt_ref, acc_ref, p_buf, v_sem, p_sem = refs[groups:]
    shards, spans, _, _ = pieces[0].shape
    units = shards * spans
    me = spot_ref[0]

    copies = []
    for r in range(groups):
        piece = lax.rem(me + r, groups)
        for s in range(shards):
            copies.append(
                pltpu.make_async_copy(
                    pieces[r].at[s], vt_ref.at[pl.ds(s * spans, spans), piece], v_sem
                )
            )
    for copy in copies:
        copy.start()

    def in_copy(chunk):
        slot = lax.rem(chunk, 2)
        return pltpu.make_async_copy(
            p_in.at[pl.ds(chunk * CHUNK, CHUNK)], p_buf.at[slot], p_sem.at[slot]
        )

    in_copy(0).start()

    def clear(unit, _):
        acc_ref[unit] = jnp.zeros(acc_ref.shape[1:], F32)
        return 0

    lax.fori_loop(0, units + 1, clear, 0)
    for copy in copies:
        copy.wait()

    def gather(j, slot, at):
        unit, key = unit_ref[LEAD + j], key_ref[LEAD + j]
        part = jnp.dot(
            vt_ref[key // groups, lax.rem(key, groups)],
            p_buf[slot, at],
            preferred_element_type=F32,
        )
        acc_ref[unit] = acc_ref[unit] * scale_ref[pl.ds(j, 1), :] + part

    chunks = (count_ref[0] + CHUNK - 1) // CHUNK

    def chunk_step(chunk, _):
        slot = lax.rem(chunk, 2)

        @pl.when(chunk + 1 < chunks)
        def _():
            in_copy(chunk + 1).start()

        in_copy(chunk).wait()

        def step(k, _):
            for i in range(VALUE_STEP):
                gather(chunk * CHUNK + VALUE_STEP * k + i, slot, VALUE_STEP * k + i)
            return 0

        lax.fori_loop(0, CHUNK // VALUE_STEP, step, 0)
        return 0

    lax.fori_loop(0, chunks, chunk_step, 0)

    def finish(i, _):
        for k in range(FINISH_STEP):
            unit = i * FINISH_STEP + k
            total = 1.0 / jnp.sum(sum_ref[unit], axis=0, keepdims=True)
            o_ref[unit] = (acc_ref[unit] * total).astype(BF16).T
        return 0

    lax.fori_loop(0, units // FINISH_STEP, finish, 0)


def attend_values(spot, jobs, pieces, probs, scales, sums):
    groups = len(pieces)
    shards, spans, _, rows = pieces[0].shape
    units = shards * spans
    work = 3 * units
    vmem = pl.BlockSpec(memory_space=pltpu.VMEM)
    return pl.pallas_call(
        functools.partial(values_kernel, groups),
        in_specs=[SMEM] * 4 + [HBM] * (groups + 1) + [vmem, vmem],
        out_specs=vmem,
        out_shape=jax.ShapeDtypeStruct((units, rows, HD), BF16),
        scratch_shapes=[
            pltpu.VMEM((units, groups, HD, rows), BF16),
            pltpu.VMEM((units + 1, HD, rows), F32),
            pltpu.VMEM((2, CHUNK, BLOCK, rows), BF16),
            pltpu.SemaphoreType.DMA,
            pltpu.SemaphoreType.DMA((2,)),
        ],
        cost_estimate=pl.CostEstimate(
            flops=2 * work * rows * BLOCK * HD,
            bytes_accessed=2 * units * groups * rows * HD + 2 * work * rows * BLOCK,
            transcendentals=0,
        ),
        name="attend_values",
    )(spot, *jobs, *pieces, probs, scales, sums)


def group_shift(x, shards, groups, r):
    pairs = [(i - i % groups + (i % groups + r) % groups, i) for i in range(shards)]
    return lax.ppermute(x, "seq", pairs)


def gather_weights(w_out, groups, member):
    count = lax.axis_size("head")
    share = w_out.shape[0] // groups
    mine = lax.dynamic_slice_in_dim(w_out, member * share, share, 0)
    return [
        lax.ppermute(mine, "head", [((i + r) % count, i) for i in range(count)])
        for r in range(1, count)
    ]


def project_kernel(spot_ref, x_ref, w_ref, *refs):
    heads, groups, spans, rows, _ = x_ref.shape
    pieces = refs[: (spans - 1) * groups]
    o_ref, wide_ref, w_buf, sem = refs[(spans - 1) * groups :]
    member, z = spot_ref[0], spot_ref[1]
    tile = w_buf.shape[2]
    share = pieces[0].shape[0]
    depth = heads * HD
    step, steps = pl.program_id(0), pl.num_programs(0)

    def copies(i):
        slot = lax.rem(i, 2)
        cols = pl.ds(pl.multiple_of(i * tile, tile), tile)
        out = [
            pltpu.make_async_copy(
                w_ref.at[:, cols],
                w_buf.at[slot, pl.ds(pl.multiple_of(z * depth, depth), depth), :],
                sem.at[slot],
            )
        ]
        for r in range(1, spans):
            for k in range(groups):
                at = lax.rem(z + r, spans) * depth + lax.rem(member + k, groups) * share
                out.append(
                    pltpu.make_async_copy(
                        pieces[(r - 1) * groups + k].at[:, cols],
                        w_buf.at[slot, pl.ds(pl.multiple_of(at, share), share), :],
                        sem.at[slot],
                    )
                )
        return out

    @pl.when(step == 0)
    def _():
        for copy in copies(step):
            copy.start()
        for z_at in range(spans):
            for h in range(heads):
                at = (z_at * heads + h) * HD
                for g in range(groups):
                    wide_ref[g * rows : (g + 1) * rows, at : at + HD] = x_ref[h, g, z_at]

    @pl.when(step + 1 < steps)
    def _():
        for copy in copies(step + 1):
            copy.start()

    for copy in copies(step):
        copy.wait()
    o_ref[...] = jnp.dot(
        wide_ref[...], w_buf[lax.rem(step, 2)], preferred_element_type=F32
    ).astype(BF16)


def project(spot, mixed, w_out, pieces):
    _, groups, spans, rows, _ = mixed.shape
    depth, width = w_out.shape
    tile = min(512, width)
    out_rows = groups * rows
    return pl.pallas_call(
        project_kernel,
        grid=(width // tile,),
        in_specs=[SMEM, pl.BlockSpec(memory_space=pltpu.VMEM)] + [HBM] * (1 + len(pieces)),
        out_specs=pl.BlockSpec((out_rows, tile), lambda i: (0, i)),
        out_shape=jax.ShapeDtypeStruct((out_rows, width), BF16),
        scratch_shapes=[
            pltpu.VMEM((out_rows, spans * depth), BF16),
            pltpu.VMEM((2, spans * depth, tile), BF16),
            pltpu.SemaphoreType.DMA((2,)),
        ],
        cost_estimate=pl.CostEstimate(
            flops=2 * out_rows * spans * depth * width,
            bytes_accessed=2 * spans * depth * width,
            transcendentals=0,
        ),
        name="project",
    )(spot, mixed, w_out, *pieces)


def body(qk, values, bucket, pair_row, pair_col, pair_count, w_out):
    shards = lax.axis_size("seq")
    spans = lax.axis_size("head")
    tokens, width = qk.shape
    heads = width // HD
    groups = shards // heads
    blocks = tokens // BLOCK
    slots = pair_row.shape[2]
    here, z = lax.axis_index("seq"), lax.axis_index("head")
    head, member = here // groups, lax.rem(here, groups)
    spot = jnp.stack([member, z, here]).astype(jnp.int32)

    shares = gather_weights(w_out, groups, member)
    units = shards * spans
    rows = tokens // spans // groups
    turned = rows == BLOCK

    def send(x, turn):
        sent = pack(x, spans, groups, turn)
        sent = sent.reshape(shards, spans, *sent.shape[3:])
        got = lax.all_to_all(sent, "seq", 0, 0, tiled=True)
        return [got] + [group_shift(got, shards, groups, r) for r in range(1, groups)]

    q_pieces = send(qk, False)
    v_pieces = send(values, turned)
    tables = gather_tables(pair_row, pair_col, pair_count, shards)
    buckets = lax.dynamic_slice_in_dim(bucket, z * heads + head, 1, 1).reshape(-1)
    jobs = job_lists(
        tables, buckets, spot, shards, slots, blocks, units, tokens // spans, rows
    )
    if turned:
        weights = attend_scores(spot, jobs, q_pieces)
        attn = attend_values(spot, jobs, v_pieces, *weights)
    else:
        attn = attend(spot, jobs, q_pieces, v_pieces)
    mixed = lax.all_to_all(attn, ("seq", "head"), 0, 0, tiled=True)
    mixed = mixed.reshape(heads, groups, spans, rows, HD)
    weights = []
    for piece in shares:
        weights += [piece] + [
            group_shift(piece, shards, groups, k) for k in range(1, groups)
        ]
    return project(spot, mixed, w_out, weights)


def solution(mesh):
    return jax.shard_map(
        body,
        mesh=mesh,
        in_specs=(
            P("seq", "head"),
            P("seq", "head"),
            P(),
            P("seq", None, None),
            P("seq", None, None),
            P("seq", None),
            P("head", None),
        ),
        out_specs=P(("seq", "head"), None),
        check_vma=False,
    )
```

```python
import functools
import math

import jax
import jax.numpy as jnp
from jax import lax
from jax.experimental import pallas as pl
from jax.experimental.pallas import tpu as pltpu
from jax.sharding import PartitionSpec as P


HD = 128
BLOCK = 256
NEG = -1e30
LEAD, TAIL = 2, 14
PREP_STEP = 4
CHUNK = 8
OUT_RING, IN_RING = 4, 8
VALUE_STEP = 4
FINISH_STEP = 4
PROJECT_TILE = 512
BF16 = jnp.bfloat16
F32 = jnp.float32
SMEM = pl.BlockSpec(memory_space=pltpu.SMEM)
HBM = pl.BlockSpec(memory_space=pl.ANY)


def pack_kernel(turned, x_ref, o_ref):
    heads, groups = o_ref.shape[:2]
    rows = x_ref.shape[0] // groups
    for h in range(heads):
        for g in range(groups):
            part = x_ref[g * rows : (g + 1) * rows, h * HD : (h + 1) * HD]
            o_ref[h, g, 0] = part.T if turned else part


def pack(x, spans, groups, turned=False):
    tokens, width = x.shape
    heads, span = width // HD, tokens // spans
    rows = span // groups
    tail = (HD, rows) if turned else (rows, HD)
    return pl.pallas_call(
        functools.partial(pack_kernel, turned),
        grid=(spans,),
        in_specs=[pl.BlockSpec((span, width), lambda i: (i, 0))],
        out_specs=pl.BlockSpec((heads, groups, 1, *tail), lambda i: (0, 0, i, 0, 0)),
        out_shape=jax.ShapeDtypeStruct((heads, groups, spans, *tail), BF16),
        cost_estimate=pl.CostEstimate(
            flops=0, bytes_accessed=4 * tokens * width, transcendentals=0
        ),
        name="pack",
    )(x)


def gather_tables(pair_row, pair_col, pair_count, shards):
    mine = jnp.concatenate(
        [pair_row.reshape(-1), pair_col.reshape(-1), pair_count.reshape(-1)]
    )
    rest = [
        lax.ppermute(mine, "seq", [((i + r) % shards, i) for i in range(shards)])
        for r in range(1, shards)
    ]
    return jnp.concatenate([mine] + rest)


def job_lists(tables, buckets, spot, shards, slots, blocks, units, span, rows):
    nblk = shards * blocks
    cap = 2 * shards * slots
    limit = job_limit(units, shards, slots)

    def kernel(tab_ref, bucket_ref, spot_ref, count_ref, unit_ref, key_ref, fill, lists):
        def clear(b, _):
            fill[b] = 0
            return 0

        lax.fori_loop(0, nblk, clear, 0)
        per = shards * slots

        def from_shard(shard, _):
            base = lax.rem(shard + shards - spot_ref[2], shards) * (2 * per + shards)

            def to_shard(other, _):
                at = base + other * slots

                def visit(slot, _):
                    a = shard * blocks + tab_ref[at + slot]
                    b = other * blocks + tab_ref[at + per + slot]

                    @pl.when(bucket_ref[a] == bucket_ref[b])
                    def _():
                        end_a, end_b = fill[a], fill[b]
                        lists[a * cap + end_a] = b
                        lists[b * cap + end_b] = a
                        fill[a] = end_a + 1
                        fill[b] = end_b + 1

                    return 0

                live = jnp.minimum(tab_ref[base + 2 * per + other], slots)
                lax.fori_loop(0, live, visit, 0)
                return 0

            lax.fori_loop(0, shards, to_shard, 0)
            return 0

        lax.fori_loop(0, shards, from_shard, 0)

        for i in range(LEAD):
            unit_ref[i] = units
            key_ref[i] = 0

        def per_unit(unit, at):
            own = (unit * span + spot_ref[0] * rows) // BLOCK
            unit_ref[at] = unit
            key_ref[at] = own
            n = fill[own]

            def partner(j, _):
                unit_ref[at + 1 + j] = unit
                key_ref[at + 1 + j] = lists[own * cap + j]
                return 0

            lax.fori_loop(0, n, partner, 0)
            return at + 1 + n

        end = lax.fori_loop(0, units, per_unit, LEAD)
        for i in range(TAIL):
            unit_ref[end + i] = units
            key_ref[end + i] = 0
        count_ref[0] = end - LEAD

    return pl.pallas_call(
        kernel,
        in_specs=[SMEM, SMEM, SMEM],
        out_specs=[SMEM, SMEM, SMEM],
        out_shape=[
            jax.ShapeDtypeStruct((1,), jnp.int32),
            jax.ShapeDtypeStruct((limit,), jnp.int32),
            jax.ShapeDtypeStruct((limit,), jnp.int32),
        ],
        scratch_shapes=[
            pltpu.SMEM((nblk,), jnp.int32),
            pltpu.SMEM((nblk * cap,), jnp.int32),
        ],
        cost_estimate=pl.CostEstimate(
            flops=0, bytes_accessed=32 * 1024 * 1024, transcendentals=0
        ),
        name="job_lists",
    )(tables, buckets, spot)


def job_limit(units, shards, slots):
    return units + 2 * shards * shards * slots + LEAD + TAIL


def attend_kernel(groups, spot_ref, count_ref, unit_ref, key_ref, *refs):
    pieces = refs[:groups], refs[groups : 2 * groups]
    refs = refs[groups:]
    o_ref, q_ref, v_ref, vt_ref, inv_ref, s0, s1, x0, x1, p0, p1, a0, a1 = refs[
        groups : groups + 13
    ]
    top_ref, sum_ref, acc_ref, q_sem, v_sem = refs[groups + 13 :]
    units, span, _ = q_ref.shape
    rows = span // groups
    spans = pieces[0][0].shape[1]
    shards = units // spans
    blocks_per = span // BLOCK
    me = spot_ref[0]
    lanes = [slice(k, min(k + HD, rows)) for k in range(0, rows, HD)]

    copies = ([], [])
    for r in range(groups):
        piece = lax.rem(me + r, groups)
        for part, ref, sem in ((0, q_ref, q_sem), (1, v_ref, v_sem)):
            for s in range(shards):
                copies[part].append(
                    pltpu.make_async_copy(
                        pieces[part][r].at[s],
                        ref.at[pl.ds(s * spans, spans), pl.ds(piece * rows, rows), :],
                        sem,
                    )
                )
    for part in copies:
        for copy in part:
            copy.start()

    def clear(unit, _):
        sum_ref[unit] = jnp.zeros(sum_ref.shape[1:], F32)
        acc_ref[unit] = jnp.zeros(acc_ref.shape[1:], F32)
        return 0

    lax.fori_loop(0, units + 1, clear, 0)
    for part in copies:
        for copy in part:
            copy.wait()

    def block_at(b):
        if blocks_per == 1:
            return b, slice(None)
        unit = b // blocks_per
        return unit, pl.ds(pl.multiple_of((b - unit * blocks_per) * BLOCK, BLOCK), BLOCK)

    ones = jnp.ones((HD, HD), BF16)
    contract = (((1,), (1,)), ((), ()))

    def prepare(i, _):
        for k in range(PREP_STEP):
            b = i * PREP_STEP + k
            unit, at = block_at(b)
            wide = q_ref[unit, at, :].astype(F32)
            square = wide * wide
            high = square.astype(BF16)
            low = (square - high.astype(F32)).astype(BF16)
            total = jnp.dot(high, ones, preferred_element_type=F32)
            total += jnp.dot(low, ones, preferred_element_type=F32)
            scale = math.log2(math.e) / math.sqrt(HD)
            inv_ref[b] = lax.rsqrt(total * (1.0 / HD) + 1e-06) * scale
            vt_ref[b] = v_ref[unit, at, :].T
        return 0

    lax.fori_loop(0, units * blocks_per // PREP_STEP, prepare, 0)

    def tiles(x):
        return x.reshape(x.shape[0] // 8, 8, x.shape[1])

    def score(t, s_ref, x_ref):
        unit, key = jnp.minimum(unit_ref[t], units - 1), key_ref[t]
        first = unit_ref[t - 1] != unit_ref[t]
        query = q_ref[unit, pl.ds(pl.multiple_of(me * rows, rows), rows), :]
        u, at = block_at(key)
        gram = lax.dot_general(q_ref[u, at, :], query, contract, preferred_element_type=F32)
        offset = lax.rem(unit * span + me * rows, BLOCK)
        shift = jnp.where(first, offset, 2 * BLOCK)
        for lane in lanes:
            n = lane.stop - lane.start
            part = gram[:, lane] * inv_ref[key, :, 0:n]
            lo, hi = (lane.start, lane.stop) if rows == BLOCK else (0, BLOCK)
            band = part[lo:hi]
            row = lax.broadcasted_iota(jnp.int32, band.shape, 0) + (lo - lane.start)
            col = lax.broadcasted_iota(jnp.int32, band.shape, 1)
            band = jnp.where(row - col == shift, NEG, band)
            above = [part[:lo]] if lo else []
            below = [part[hi:]] if hi < BLOCK else []
            part = jnp.concatenate(above + [band] + below, axis=0)
            s_ref[:, lane] = part
            most = jnp.max(jnp.max(tiles(part), axis=0), axis=0, keepdims=True)
            x_ref[:, lane] = jnp.broadcast_to(most, (8, n))

    def weigh(t, s_ref, x_ref, p_ref, a_ref):
        unit = unit_ref[t]
        first = unit_ref[t - 1] != unit
        old = jnp.where(first, 2 * NEG, top_ref[...])
        new = jnp.maximum(old, x_ref[...])
        top_ref[...] = new
        scale = jnp.exp2(old - new)
        a_ref[...] = scale
        for lane in lanes:
            prob = jnp.exp2(tiles(s_ref[:, lane]) - new[None, :, lane])
            sum_ref[unit, :, lane] = sum_ref[unit, :, lane] * scale[:, lane] + jnp.sum(
                prob, axis=0
            )
            p_ref[:, lane] = prob.reshape(BLOCK, lane.stop - lane.start).astype(BF16)

    def gather(t, p_ref, a_ref):
        unit, key = unit_ref[t], key_ref[t]
        part = jnp.dot(vt_ref[key], p_ref[...], preferred_element_type=F32)
        kept = tiles(acc_ref[unit]) * a_ref[...][None]
        acc_ref[unit] = kept.reshape(HD, rows) + part

    def pair_step(i, _):
        t = LEAD + 2 * i
        gather(t - 2, p0, a0)
        weigh(t - 1, s1, x1, p1, a1)
        score(t, s0, x0)
        gather(t - 1, p1, a1)
        weigh(t, s0, x0, p0, a0)
        score(t + 1, s1, x1)
        return 0

    lax.fori_loop(0, (count_ref[0] + 1) // 2 + 1, pair_step, 0)

    def finish(unit, _):
        total = 1.0 / jnp.sum(sum_ref[unit], axis=0, keepdims=True)
        o_ref[unit] = (acc_ref[unit] * total).T.astype(BF16)
        return 0

    lax.fori_loop(0, units, finish, 0)


def attend(spot, jobs, q_pieces, v_pieces):
    groups = len(q_pieces)
    shards, spans, rows, _ = q_pieces[0].shape
    units, span = shards * spans, rows * groups
    nblk = units * span // BLOCK
    work = 3 * units
    scores = pltpu.VMEM((BLOCK, rows), F32)
    probs = pltpu.VMEM((BLOCK, rows), BF16)
    line = pltpu.VMEM((8, rows), F32)
    return pl.pallas_call(
        functools.partial(attend_kernel, groups),
        in_specs=[SMEM] * 4 + [HBM] * (2 * groups),
        out_specs=pl.BlockSpec(memory_space=pltpu.VMEM),
        out_shape=jax.ShapeDtypeStruct((units, rows, HD), BF16),
        scratch_shapes=[
            pltpu.VMEM((units, span, HD), BF16),
            pltpu.VMEM((units, span, HD), BF16),
            pltpu.VMEM((nblk, HD, BLOCK), BF16),
            pltpu.VMEM((nblk, BLOCK, HD), F32),
            *[scores, scores, line, line, probs, probs, line, line],
            line,
            pltpu.VMEM((units + 1, 8, rows), F32),
            pltpu.VMEM((units + 1, HD, rows), F32),
            pltpu.SemaphoreType.DMA,
            pltpu.SemaphoreType.DMA,
        ],
        cost_estimate=pl.CostEstimate(
            flops=4 * work * rows * BLOCK * HD,
            bytes_accessed=4 * units * span * HD,
            transcendentals=work * rows * BLOCK,
        ),
        name="attend",
    )(spot, *jobs, *q_pieces, *v_pieces)


def scores_kernel(groups, spot_ref, count_ref, unit_ref, key_ref, *refs):
    pieces = refs[:groups]
    p_out, scale_ref, sum_ref, q_ref, inv_ref, s0, s1, x0, x1, top_ref, p_buf, q_sem, p_sem = refs[
        groups:
    ]
    shards, spans, rows, _ = pieces[0].shape
    units = shards * spans
    me = spot_ref[0]
    lanes = [slice(k, k + HD) for k in range(0, rows, HD)]

    copies = []
    for r in range(groups):
        piece = lax.rem(me + r, groups)
        for s in range(shards):
            copies.append(
                pltpu.make_async_copy(
                    pieces[r].at[s], q_ref.at[pl.ds(s * spans, spans), piece], q_sem
                )
            )
    for copy in copies:
        copy.start()
    sum_ref[...] = jnp.zeros(sum_ref.shape, F32)
    for copy in copies:
        copy.wait()

    contract = (((1,), (1,)), ((), ()))
    fold = math.log2(math.e) ** -2

    def prepare(i, _):
        for k in range(PREP_STEP):
            b = i * PREP_STEP + k
            wide = q_ref[b // groups, lax.rem(b, groups)].astype(F32)
            total = jnp.sum(wide * wide, axis=1, keepdims=True)
            inv = lax.rsqrt(total * fold + 1e-06 * HD * fold)
            inv_ref[b] = jnp.broadcast_to(inv, (BLOCK, HD))
        return 0

    lax.fori_loop(0, units * groups // PREP_STEP, prepare, 0)

    def tiles(x):
        return x.reshape(x.shape[0] // 8, 8, x.shape[1])

    def score(j, s_ref, x_ref):
        t = LEAD + j
        unit, key = jnp.minimum(unit_ref[t], units - 1), key_ref[t]
        first = unit_ref[t - 1] != unit_ref[t]
        gram = lax.dot_general(
            q_ref[key // groups, lax.rem(key, groups)],
            q_ref[unit, me],
            contract,
            preferred_element_type=F32,
        )
        shift = jnp.where(first, 0, 2 * BLOCK)
        for lane in lanes:
            part = gram[:, lane] * inv_ref[key]
            band = part[lane]
            row = lax.broadcasted_iota(jnp.int32, band.shape, 0)
            col = lax.broadcasted_iota(jnp.int32, band.shape, 1)
            band = jnp.where(row - col == shift, NEG, band)
            above = [part[: lane.start]] if lane.start else []
            below = [part[lane.stop :]] if lane.stop < BLOCK else []
            part = jnp.concatenate(above + [band] + below, axis=0)
            s_ref[:, lane] = part
            most = jnp.max(jnp.max(tiles(part), axis=0), axis=0, keepdims=True)
            x_ref[:, lane] = jnp.broadcast_to(most, (8, HD))

    def weigh(j, s_ref, x_ref, slot, at):
        unit = unit_ref[LEAD + j]
        first = unit_ref[LEAD + j - 1] != unit
        old = jnp.where(first, 2 * NEG, top_ref[...])
        new = jnp.maximum(old, x_ref[...])
        top_ref[...] = new
        scale = jnp.exp2(old - new)
        scale_ref[pl.ds(j, 1), :] = scale[0:1]
        total = sum_ref[unit] * scale
        for lane in lanes:
            prob = jnp.exp2(tiles(s_ref[:, lane]) - new[None, :, lane])
            sum_ref[unit, :, lane] = total[:, lane] + jnp.sum(prob, axis=0)
            p_buf[slot, at, :, lane] = prob.reshape(BLOCK, HD).astype(BF16)

    ring = p_buf.shape[0]

    def out_copy(chunk):
        slot = lax.rem(chunk, ring)
        return pltpu.make_async_copy(
            p_buf.at[slot], p_out.at[pl.ds(chunk * CHUNK, CHUNK)], p_sem.at[slot]
        )

    score(0, s0, x0)
    score(1, s1, x1)
    chunks = (count_ref[0] + CHUNK - 1) // CHUNK

    def chunk_step(chunk, _):
        slot = lax.rem(chunk, ring)

        @pl.when(chunk >= ring)
        def _():
            out_copy(chunk - ring).wait()

        def step(k, _):
            j = chunk * CHUNK + 2 * k
            weigh(j, s0, x0, slot, 2 * k)
            weigh(j + 1, s1, x1, slot, 2 * k + 1)
            score(j + 2, s0, x0)
            score(j + 3, s1, x1)
            return 0

        lax.fori_loop(0, CHUNK // 2, step, 0)
        out_copy(chunk).start()
        return 0

    lax.fori_loop(0, chunks, chunk_step, 0)
    for back in range(ring, 0, -1):

        @pl.when(chunks >= back)
        def _():
            out_copy(chunks - back).wait()


def attend_scores(spot, jobs, pieces):
    groups = len(pieces)
    shards, spans, rows, _ = pieces[0].shape
    units = shards * spans
    nblk = units * groups
    room = jobs[1].shape[0] // CHUNK * CHUNK
    work = 3 * units
    vmem = pl.BlockSpec(memory_space=pltpu.VMEM)
    return pl.pallas_call(
        functools.partial(scores_kernel, groups),
        in_specs=[SMEM] * 4 + [HBM] * groups,
        out_specs=[HBM, vmem, vmem],
        out_shape=[
            jax.ShapeDtypeStruct((room, BLOCK, rows), BF16),
            jax.ShapeDtypeStruct((room, rows), F32),
            jax.ShapeDtypeStruct((units + 1, 8, rows), F32),
        ],
        scratch_shapes=[
            pltpu.VMEM((units, groups, rows, HD), BF16),
            pltpu.VMEM((nblk, BLOCK, HD), F32),
            pltpu.VMEM((BLOCK, rows), F32),
            pltpu.VMEM((BLOCK, rows), F32),
            *[pltpu.VMEM((8, rows), F32)] * 3,
            pltpu.VMEM((OUT_RING, CHUNK, BLOCK, rows), BF16),
            pltpu.SemaphoreType.DMA,
            pltpu.SemaphoreType.DMA((OUT_RING,)),
        ],
        cost_estimate=pl.CostEstimate(
            flops=2 * work * rows * BLOCK * HD,
            bytes_accessed=2 * units * groups * rows * HD + 2 * work * rows * BLOCK,
            transcendentals=work * rows * BLOCK,
        ),
        name="attend_scores",
    )(spot, *jobs, *pieces)


def values_kernel(groups, spot_ref, count_ref, unit_ref, key_ref, *refs):
    pieces = refs[:groups]
    p_in, scale_ref, sum_ref, o_ref, vt_ref, acc_ref, p_buf, v_sem, p_sem = refs[groups:]
    shards, spans, _, _ = pieces[0].shape
    units = shards * spans
    me = spot_ref[0]

    copies = []
    for r in range(groups):
        piece = lax.rem(me + r, groups)
        for s in range(shards):
            copies.append(
                pltpu.make_async_copy(
                    pieces[r].at[s], vt_ref.at[pl.ds(s * spans, spans), piece], v_sem
                )
            )
    for copy in copies:
        copy.start()

    ring = p_buf.shape[0]
    chunks = (count_ref[0] + CHUNK - 1) // CHUNK

    def in_copy(chunk):
        slot = lax.rem(chunk, ring)
        return pltpu.make_async_copy(
            p_in.at[pl.ds(chunk * CHUNK, CHUNK)], p_buf.at[slot], p_sem.at[slot]
        )

    for ahead in range(ring - 1):

        @pl.when(ahead < chunks)
        def _():
            in_copy(ahead).start()

    def clear(unit, _):
        acc_ref[unit] = jnp.zeros(acc_ref.shape[1:], F32)
        return 0

    lax.fori_loop(0, units + 1, clear, 0)
    for copy in copies:
        copy.wait()

    def gather(j, slot, at):
        unit, key = unit_ref[LEAD + j], key_ref[LEAD + j]
        part = jnp.dot(
            vt_ref[key // groups, lax.rem(key, groups)],
            p_buf[slot, at],
            preferred_element_type=F32,
        )
        acc_ref[unit] = acc_ref[unit] * scale_ref[pl.ds(j, 1), :] + part

    def chunk_step(chunk, _):
        slot = lax.rem(chunk, ring)

        @pl.when(chunk + ring - 1 < chunks)
        def _():
            in_copy(chunk + ring - 1).start()

        in_copy(chunk).wait()

        def step(k, _):
            for i in range(VALUE_STEP):
                gather(chunk * CHUNK + VALUE_STEP * k + i, slot, VALUE_STEP * k + i)
            return 0

        lax.fori_loop(0, CHUNK // VALUE_STEP, step, 0)
        return 0

    lax.fori_loop(0, chunks, chunk_step, 0)

    def finish(i, _):
        for k in range(FINISH_STEP):
            unit = i * FINISH_STEP + k
            total = 1.0 / jnp.sum(sum_ref[unit], axis=0, keepdims=True)
            o_ref[unit] = (acc_ref[unit] * total).astype(BF16).T
        return 0

    lax.fori_loop(0, units // FINISH_STEP, finish, 0)


def attend_values(spot, jobs, pieces, probs, scales, sums):
    groups = len(pieces)
    shards, spans, _, rows = pieces[0].shape
    units = shards * spans
    work = 3 * units
    vmem = pl.BlockSpec(memory_space=pltpu.VMEM)
    return pl.pallas_call(
        functools.partial(values_kernel, groups),
        in_specs=[SMEM] * 4 + [HBM] * (groups + 1) + [vmem, vmem],
        out_specs=vmem,
        out_shape=jax.ShapeDtypeStruct((units, rows, HD), BF16),
        scratch_shapes=[
            pltpu.VMEM((units, groups, HD, rows), BF16),
            pltpu.VMEM((units + 1, HD, rows), F32),
            pltpu.VMEM((IN_RING, CHUNK, BLOCK, rows), BF16),
            pltpu.SemaphoreType.DMA,
            pltpu.SemaphoreType.DMA((IN_RING,)),
        ],
        cost_estimate=pl.CostEstimate(
            flops=2 * work * rows * BLOCK * HD,
            bytes_accessed=2 * units * groups * rows * HD + 2 * work * rows * BLOCK,
            transcendentals=0,
        ),
        name="attend_values",
    )(spot, *jobs, *pieces, probs, scales, sums)


def group_shift(x, shards, groups, r):
    pairs = [(i - i % groups + (i % groups + r) % groups, i) for i in range(shards)]
    return lax.ppermute(x, "seq", pairs)


def ring_weights(w_out, groups, member):
    count = lax.axis_size("head")
    here = lax.axis_index("head")
    share = w_out.shape[0] // groups
    up = down = lax.dynamic_slice_in_dim(w_out, member * share, share, 0)
    ups, downs = {}, {}
    for k in range(1, count):
        up = lax.ppermute(up, "head", [(i, i + 1) for i in range(k - 1, count - 1)])
        down = lax.ppermute(down, "head", [(i, i - 1) for i in range(1, count - k + 1)])
        ups[k], downs[k] = up, down
    return [
        jnp.where(here + r < count, downs[r], ups[count - r]) for r in range(1, count)
    ]


def project_kernel(spot_ref, x_ref, w_ref, *refs):
    heads, groups, spans, rows, _ = x_ref.shape
    pieces = refs[: (spans - 1) * groups]
    o_ref, wide_ref, w_buf, sem = refs[(spans - 1) * groups :]
    member, z = spot_ref[0], spot_ref[1]
    tile = w_buf.shape[2]
    share = pieces[0].shape[0]
    depth = heads * HD
    step = pl.program_id(0)

    def copies(slot):
        cols = pl.ds(slot * tile, tile)
        if not isinstance(slot, int):
            cols = pl.ds(pl.multiple_of(slot * tile, tile), tile)
        out = [
            pltpu.make_async_copy(
                w_ref.at[:, cols],
                w_buf.at[slot, pl.ds(pl.multiple_of(z * depth, depth), depth), :],
                sem.at[slot],
            )
        ]
        for r in range(1, spans):
            for k in range(groups):
                at = lax.rem(z + r, spans) * depth + lax.rem(member + k, groups) * share
                out.append(
                    pltpu.make_async_copy(
                        pieces[(r - 1) * groups + k].at[:, cols],
                        w_buf.at[slot, pl.ds(pl.multiple_of(at, share), share), :],
                        sem.at[slot],
                    )
                )
        return out

    @pl.when(step == 0)
    def _():
        for i in range(w_buf.shape[0]):
            for copy in copies(i):
                copy.start()
        for z_at in range(spans):
            for h in range(heads):
                at = (z_at * heads + h) * HD
                for g in range(groups):
                    wide_ref[g * rows : (g + 1) * rows, at : at + HD] = x_ref[h, g, z_at]

    for copy in copies(step):
        copy.wait()
    o_ref[...] = jnp.dot(wide_ref[...], w_buf[step], preferred_element_type=F32).astype(BF16)


def project(spot, mixed, w_out, pieces):
    _, groups, spans, rows, _ = mixed.shape
    depth, width = w_out.shape
    tile = min(PROJECT_TILE, width)
    out_rows = groups * rows
    return pl.pallas_call(
        project_kernel,
        grid=(width // tile,),
        in_specs=[SMEM, pl.BlockSpec(memory_space=pltpu.VMEM)] + [HBM] * (1 + len(pieces)),
        out_specs=pl.BlockSpec((out_rows, tile), lambda i: (0, i)),
        out_shape=jax.ShapeDtypeStruct((out_rows, width), BF16),
        scratch_shapes=[
            pltpu.VMEM((out_rows, spans * depth), BF16),
            pltpu.VMEM((width // tile, spans * depth, tile), BF16),
            pltpu.SemaphoreType.DMA((width // tile,)),
        ],
        cost_estimate=pl.CostEstimate(
            flops=2 * out_rows * spans * depth * width,
            bytes_accessed=2 * spans * depth * width,
            transcendentals=0,
        ),
        name="project",
    )(spot, pltpu.with_memory_space_constraint(mixed, pltpu.VMEM), w_out, *pieces)


def body(qk, values, bucket, pair_row, pair_col, pair_count, w_out):
    shards = lax.axis_size("seq")
    spans = lax.axis_size("head")
    tokens, width = qk.shape
    heads = width // HD
    groups = shards // heads
    blocks = tokens // BLOCK
    slots = pair_row.shape[2]
    here, z = lax.axis_index("seq"), lax.axis_index("head")
    head, member = here // groups, lax.rem(here, groups)
    spot = jnp.stack([member, z, here]).astype(jnp.int32)

    shares = ring_weights(w_out, groups, member)
    units = shards * spans
    rows = tokens // spans // groups
    turned = rows == BLOCK

    def send(x, turn):
        sent = pack(x, spans, groups, turn)
        sent = sent.reshape(shards, spans, *sent.shape[3:])
        got = lax.all_to_all(sent, "seq", 0, 0, tiled=True)
        return [got] + [group_shift(got, shards, groups, r) for r in range(1, groups)]

    q_pieces = send(qk, False)
    v_pieces = send(values, turned)
    tables = gather_tables(pair_row, pair_col, pair_count, shards)
    buckets = lax.dynamic_slice_in_dim(bucket, z * heads + head, 1, 1).reshape(-1)
    jobs = job_lists(
        tables, buckets, spot, shards, slots, blocks, units, tokens // spans, rows
    )
    if turned:
        weights = attend_scores(spot, jobs, q_pieces)
        v_pieces = [pltpu.with_memory_space_constraint(x, pltpu.HBM) for x in v_pieces]
        attn = attend_values(spot, jobs, v_pieces, *weights)
    else:
        attn = attend(spot, jobs, q_pieces, v_pieces)
    mixed = lax.all_to_all(attn, ("seq", "head"), 0, 0, tiled=True)
    mixed = mixed.reshape(heads, groups, spans, rows, HD)
    weights = []
    shares = [pltpu.with_memory_space_constraint(x, pltpu.HBM) for x in shares]
    for piece in shares:
        weights += [piece] + [
            group_shift(piece, shards, groups, k) for k in range(1, groups)
        ]
    weights = [pltpu.with_memory_space_constraint(x, pltpu.HBM) for x in weights]
    return project(spot, mixed, w_out, weights)


def solution(mesh):
    return jax.shard_map(
        body,
        mesh=mesh,
        in_specs=(
            P("seq", "head"),
            P("seq", "head"),
            P(),
            P("seq", None, None),
            P("seq", None, None),
            P("seq", None),
            P("head", None),
        ),
        out_specs=P(("seq", "head"), None),
        check_vma=False,
    )
```

```python
import functools
import math

import jax
import jax.numpy as jnp
from jax import lax
from jax.experimental import pallas as pl
from jax.experimental.pallas import tpu as pltpu
from jax.sharding import PartitionSpec as P


HD = 128
BLOCK = 256
NEG = -1e30
MIB = 1024 * 1024
LEAD, TAIL = 2, 14
PREP_STEP = 4
CHUNK = 8
OUT_RING, IN_RING = 4, 8
SCORE_STEP = 4
VALUE_STEP = 8
ONES = 16
FINISH_STEP = 4
PROJECT_TILE = 512
BF16 = jnp.bfloat16
F32 = jnp.float32
SMEM = pl.BlockSpec(memory_space=pltpu.SMEM)
HBM = pl.BlockSpec(memory_space=pl.ANY)


def turn_kernel(x_ref, o_ref):
    heads, groups = o_ref.shape[:2]
    rows = x_ref.shape[0] // groups
    for h in range(heads):
        for g in range(groups):
            o_ref[h, g, 0] = x_ref[g * rows : (g + 1) * rows, h * HD : (h + 1) * HD].T


def pack_kernel(x_ref, o_ref, held_ref, in_sem, out_sem):
    heads, groups, spans, rows, _ = o_ref.shape
    steps = [(z, g) for z in range(spans) for g in range(groups)]

    def arrive(i):
        some = pl.ds(i * rows, rows)
        return pltpu.make_async_copy(x_ref.at[some], held_ref.at[some], in_sem.at[i])

    def leave(i, h):
        z, g = steps[i]
        return pltpu.make_async_copy(
            held_ref.at[pl.ds(i * rows, rows), pl.ds(h * HD, HD)],
            o_ref.at[h, g, z],
            out_sem.at[i, h],
        )

    for i in range(len(steps)):
        arrive(i).start()
    for i in range(len(steps)):
        arrive(i).wait()
        for h in range(heads):
            leave(i, h).start()
    for i in range(len(steps)):
        for h in range(heads):
            leave(i, h).wait()


def pack(x, spans, groups, turned=False):
    tokens, width = x.shape
    heads, span = width // HD, tokens // spans
    rows = span // groups
    cost = pl.CostEstimate(flops=0, bytes_accessed=4 * tokens * width, transcendentals=0)
    if turned:
        return pl.pallas_call(
            turn_kernel,
            grid=(spans,),
            in_specs=[pl.BlockSpec((span, width), lambda i: (i, 0))],
            out_specs=pl.BlockSpec((heads, groups, 1, HD, rows), lambda i: (0, 0, i, 0, 0)),
            out_shape=jax.ShapeDtypeStruct((heads, groups, spans, HD, rows), BF16),
            cost_estimate=cost,
            name="turn",
        )(x)
    return pl.pallas_call(
        pack_kernel,
        in_specs=[HBM],
        out_specs=HBM,
        out_shape=jax.ShapeDtypeStruct((heads, groups, spans, rows, HD), BF16),
        scratch_shapes=[
            pltpu.VMEM((tokens, width), BF16),
            pltpu.SemaphoreType.DMA((spans * groups,)),
            pltpu.SemaphoreType.DMA((spans * groups, heads)),
        ],
        cost_estimate=cost,
        name="pack",
    )(x)


def gather_tables(pair_row, pair_col, pair_count, shards):
    mine = jnp.concatenate(
        [pair_row.reshape(-1), pair_col.reshape(-1), pair_count.reshape(-1)]
    )
    rest = [
        lax.ppermute(mine, "seq", [((i + r) % shards, i) for i in range(shards)])
        for r in range(1, shards)
    ]
    return jnp.concatenate([mine] + rest)


def job_lists(tables, bucket, spot, shards, slots, blocks, units, span, rows):
    nblk = shards * blocks
    cap = 2 * shards * slots
    limit = job_limit(units, shards, slots)

    def kernel(tab_ref, bucket_ref, spot_ref, count_ref, unit_ref, key_ref, fill, lists):
        head = spot_ref[3]

        def clear(b, _):
            fill[b] = 0
            return 0

        lax.fori_loop(0, nblk, clear, 0)
        per = shards * slots

        for r in range(shards):
            shard = lax.rem(spot_ref[2] + r, shards)
            base = r * (2 * per + shards)

            def to_shard(other, _):
                at = base + other * slots

                def visit(slot, _):
                    a = shard * blocks + tab_ref[at + slot]
                    b = other * blocks + tab_ref[at + per + slot]

                    @pl.when(bucket_ref[head, a] == bucket_ref[head, b])
                    def _():
                        end_a, end_b = fill[a], fill[b]
                        lists[a * cap + end_a] = b
                        lists[b * cap + end_b] = a
                        fill[a] = end_a + 1
                        fill[b] = end_b + 1

                    return 0

                live = jnp.minimum(tab_ref[base + 2 * per + other], slots)
                lax.fori_loop(0, live, visit, 0)
                return 0

            lax.fori_loop(0, shards, to_shard, 0)

        for i in range(LEAD):
            unit_ref[i] = units
            key_ref[i] = 0

        def per_unit(unit, at):
            own = (unit * span + spot_ref[0] * rows) // BLOCK
            unit_ref[at] = unit
            key_ref[at] = own
            n = fill[own]

            def partner(j, _):
                unit_ref[at + 1 + j] = unit
                key_ref[at + 1 + j] = lists[own * cap + j]
                return 0

            lax.fori_loop(0, n, partner, 0)
            return at + 1 + n

        end = lax.fori_loop(0, units, per_unit, LEAD)
        for i in range(TAIL):
            unit_ref[end + i] = units
            key_ref[end + i] = 0
        count_ref[0] = end - LEAD

    return pl.pallas_call(
        kernel,
        in_specs=[SMEM] * 3,
        out_specs=[SMEM, SMEM, SMEM],
        out_shape=[
            jax.ShapeDtypeStruct((1,), jnp.int32),
            jax.ShapeDtypeStruct((limit,), jnp.int32),
            jax.ShapeDtypeStruct((limit,), jnp.int32),
        ],
        scratch_shapes=[
            pltpu.SMEM((nblk,), jnp.int32),
            pltpu.SMEM((nblk * cap,), jnp.int32),
        ],
        cost_estimate=pl.CostEstimate(
            flops=0, bytes_accessed=32 * 1024 * 1024, transcendentals=0
        ),
        name="job_lists",
    )(tables, bucket.T, spot)


def job_limit(units, shards, slots):
    return units + 2 * shards * shards * slots + LEAD + TAIL


def attend_kernel(groups, spot_ref, count_ref, unit_ref, key_ref, *refs):
    pieces = refs[:groups], refs[groups : 2 * groups]
    refs = refs[groups:]
    o_ref, q_ref, v_ref, vt_ref, inv_ref, s0, s1, x0, x1, p0, p1, a0, a1 = refs[
        groups : groups + 13
    ]
    top_ref, sum_ref, acc_ref, q_sem, v_sem = refs[groups + 13 :]
    units, span, _ = q_ref.shape
    rows = span // groups
    spans = pieces[0][0].shape[1]
    shards = units // spans
    blocks_per = span // BLOCK
    me = spot_ref[0]
    lanes = [slice(k, min(k + HD, rows)) for k in range(0, rows, HD)]

    copies = ([], [])
    for r in range(groups):
        piece = lax.rem(me + r, groups)
        for part, ref, sem in ((0, q_ref, q_sem), (1, v_ref, v_sem)):
            for s in range(shards):
                copies[part].append(
                    pltpu.make_async_copy(
                        pieces[part][r].at[s],
                        ref.at[pl.ds(s * spans, spans), pl.ds(piece * rows, rows), :],
                        sem,
                    )
                )
    for part in copies:
        for copy in part:
            copy.start()

    def clear(unit, _):
        sum_ref[unit] = jnp.zeros(sum_ref.shape[1:], F32)
        acc_ref[unit] = jnp.zeros(acc_ref.shape[1:], F32)
        return 0

    lax.fori_loop(0, units + 1, clear, 0)
    for part in copies:
        for copy in part:
            copy.wait()

    def block_at(b):
        if blocks_per == 1:
            return b, slice(None)
        unit = b // blocks_per
        return unit, pl.ds(pl.multiple_of((b - unit * blocks_per) * BLOCK, BLOCK), BLOCK)

    ones = jnp.ones((HD, HD), BF16)
    contract = (((1,), (1,)), ((), ()))

    def prepare(i, _):
        for k in range(PREP_STEP):
            b = i * PREP_STEP + k
            unit, at = block_at(b)
            wide = q_ref[unit, at, :].astype(F32)
            square = wide * wide
            high = square.astype(BF16)
            low = (square - high.astype(F32)).astype(BF16)
            total = jnp.dot(high, ones, preferred_element_type=F32)
            total += jnp.dot(low, ones, preferred_element_type=F32)
            scale = math.log2(math.e) / math.sqrt(HD)
            inv_ref[b] = lax.rsqrt(total * (1.0 / HD) + 1e-06) * scale
            vt_ref[b] = v_ref[unit, at, :].T
        return 0

    lax.fori_loop(0, units * blocks_per // PREP_STEP, prepare, 0)

    def tiles(x):
        return x.reshape(x.shape[0] // 8, 8, x.shape[1])

    def score(t, s_ref, x_ref):
        unit, key = jnp.minimum(unit_ref[t], units - 1), key_ref[t]
        first = unit_ref[t - 1] != unit_ref[t]
        query = q_ref[unit, pl.ds(pl.multiple_of(me * rows, rows), rows), :]
        u, at = block_at(key)
        gram = lax.dot_general(q_ref[u, at, :], query, contract, preferred_element_type=F32)
        offset = lax.rem(unit * span + me * rows, BLOCK)
        shift = jnp.where(first, offset, 2 * BLOCK)
        for lane in lanes:
            n = lane.stop - lane.start
            part = gram[:, lane] * inv_ref[key, :, 0:n]
            lo, hi = (lane.start, lane.stop) if rows == BLOCK else (0, BLOCK)
            band = part[lo:hi]
            row = lax.broadcasted_iota(jnp.int32, band.shape, 0) + (lo - lane.start)
            col = lax.broadcasted_iota(jnp.int32, band.shape, 1)
            band = jnp.where(row - col == shift, NEG, band)
            above = [part[:lo]] if lo else []
            below = [part[hi:]] if hi < BLOCK else []
            part = jnp.concatenate(above + [band] + below, axis=0)
            s_ref[:, lane] = part
            most = jnp.max(jnp.max(tiles(part), axis=0), axis=0, keepdims=True)
            x_ref[:, lane] = jnp.broadcast_to(most, (8, n))

    def weigh(t, s_ref, x_ref, p_ref, a_ref):
        unit = unit_ref[t]
        first = unit_ref[t - 1] != unit
        old = jnp.where(first, 2 * NEG, top_ref[...])
        new = jnp.maximum(old, x_ref[...])
        top_ref[...] = new
        scale = jnp.exp2(old - new)
        a_ref[...] = scale
        for lane in lanes:
            prob = jnp.exp2(tiles(s_ref[:, lane]) - new[None, :, lane])
            sum_ref[unit, :, lane] = sum_ref[unit, :, lane] * scale[:, lane] + jnp.sum(
                prob, axis=0
            )
            p_ref[:, lane] = prob.reshape(BLOCK, lane.stop - lane.start).astype(BF16)

    def gather(t, p_ref, a_ref):
        unit, key = unit_ref[t], key_ref[t]
        part = jnp.dot(vt_ref[key], p_ref[...], preferred_element_type=F32)
        kept = tiles(acc_ref[unit]) * a_ref[...][None]
        acc_ref[unit] = kept.reshape(HD, rows) + part

    def pair_step(i, _):
        t = LEAD + 2 * i
        gather(t - 2, p0, a0)
        weigh(t - 1, s1, x1, p1, a1)
        score(t, s0, x0)
        gather(t - 1, p1, a1)
        weigh(t, s0, x0, p0, a0)
        score(t + 1, s1, x1)
        return 0

    lax.fori_loop(0, (count_ref[0] + 1) // 2 + 1, pair_step, 0)

    def finish(unit, _):
        total = 1.0 / jnp.sum(sum_ref[unit], axis=0, keepdims=True)
        o_ref[unit] = (acc_ref[unit] * total).T.astype(BF16)
        return 0

    lax.fori_loop(0, units, finish, 0)


def attend(spot, jobs, q_pieces, v_pieces):
    groups = len(q_pieces)
    shards, spans, rows, _ = q_pieces[0].shape
    units, span = shards * spans, rows * groups
    nblk = units * span // BLOCK
    work = 3 * units
    scores = pltpu.VMEM((BLOCK, rows), F32)
    probs = pltpu.VMEM((BLOCK, rows), BF16)
    line = pltpu.VMEM((8, rows), F32)
    return pl.pallas_call(
        functools.partial(attend_kernel, groups),
        in_specs=[SMEM] * 4 + [HBM] * (2 * groups),
        out_specs=pl.BlockSpec(memory_space=pltpu.VMEM),
        out_shape=jax.ShapeDtypeStruct((units, rows, HD), BF16),
        scratch_shapes=[
            pltpu.VMEM((units, span, HD), BF16),
            pltpu.VMEM((units, span, HD), BF16),
            pltpu.VMEM((nblk, HD, BLOCK), BF16),
            pltpu.VMEM((nblk, BLOCK, HD), F32),
            *[scores, scores, line, line, probs, probs, line, line],
            line,
            pltpu.VMEM((units + 1, 8, rows), F32),
            pltpu.VMEM((units + 1, HD, rows), F32),
            pltpu.SemaphoreType.DMA,
            pltpu.SemaphoreType.DMA,
        ],
        cost_estimate=pl.CostEstimate(
            flops=4 * work * rows * BLOCK * HD,
            bytes_accessed=4 * units * span * HD,
            transcendentals=work * rows * BLOCK,
        ),
        name="attend",
    )(spot, *jobs, *q_pieces, *v_pieces)


def scores_kernel(groups, spot_ref, count_ref, unit_ref, key_ref, *refs):
    pieces = refs[:groups]
    p_out, scale_ref, q_ref, inv_ref, top_ref, p_buf, q_sem, p_sem = refs[groups : groups + 8]
    held = refs[groups + 8 :]
    s_refs, x_refs = held[:SCORE_STEP], held[SCORE_STEP:]
    shards, spans, rows, _ = pieces[0].shape
    units = shards * spans
    me = spot_ref[0]
    lanes = [slice(k, k + HD) for k in range(0, rows, HD)]

    def arrivals(s):
        some = pl.ds(s * spans, spans)
        return [
            pltpu.make_async_copy(
                pieces[r].at[s], q_ref.at[some, lax.rem(me + r, groups)], q_sem.at[s]
            )
            for r in range(groups)
        ]

    for s in range(shards):
        for copy in arrivals(s):
            copy.start()

    fold = math.log2(math.e) ** -2

    def prepare(s, _):
        for copy in arrivals(s):
            copy.wait()
        for k in range(spans * groups):
            unit, piece = s * spans + k // groups, k % groups
            wide = q_ref[unit, piece].astype(F32)
            total = jnp.sum(wide * wide, axis=1, keepdims=True)
            inv = lax.rsqrt(total * fold + 1e-06 * HD * fold)
            inv_ref[unit * groups + piece] = jnp.broadcast_to(inv, (BLOCK, HD))
        return 0

    lax.fori_loop(0, shards, prepare, 0)

    def tiles(x):
        return x.reshape(x.shape[0] // 8, 8, x.shape[1])

    def score(j, s_ref, x_ref):
        t = LEAD + j
        unit, key = jnp.minimum(unit_ref[t], units - 1), key_ref[t]
        first = unit_ref[t - 1] != unit_ref[t]
        gram = lax.dot_general(
            q_ref[key // groups, lax.rem(key, groups)],
            q_ref[unit, me],
            (((1,), (1,)), ((), ())),
            preferred_element_type=F32,
        )
        shift = jnp.where(first, 0, 2 * BLOCK)
        for lane in lanes:
            part = gram[:, lane] * inv_ref[key]
            band = part[lane]
            row = lax.broadcasted_iota(jnp.int32, band.shape, 0)
            col = lax.broadcasted_iota(jnp.int32, band.shape, 1)
            band = jnp.where(row - col == shift, NEG, band)
            above = [part[: lane.start]] if lane.start else []
            below = [part[lane.stop :]] if lane.stop < BLOCK else []
            part = jnp.concatenate(above + [band] + below, axis=0)
            s_ref[:, lane] = part
            most = jnp.max(jnp.max(tiles(part), axis=0), axis=0, keepdims=True)
            x_ref[:, lane] = jnp.broadcast_to(most, (8, HD))

    def weigh(j, s_ref, x_ref, slot, at):
        first = unit_ref[LEAD + j - 1] != unit_ref[LEAD + j]
        old = jnp.where(first, 2 * NEG, top_ref[...])
        new = jnp.maximum(old, x_ref[...])
        top_ref[...] = new
        scale_ref[pl.ds(j, 1), :] = jnp.exp2(old - new)[0:1]
        for lane in lanes:
            prob = jnp.exp2(tiles(s_ref[:, lane]) - new[None, :, lane])
            p_buf[slot, at, :, lane] = prob.reshape(BLOCK, HD).astype(BF16)

    def out_copy(chunk):
        slot = lax.rem(chunk, OUT_RING)
        return pltpu.make_async_copy(
            p_buf.at[slot], p_out.at[pl.ds(chunk * CHUNK, CHUNK)], p_sem.at[slot]
        )

    for i in range(SCORE_STEP):
        score(i, s_refs[i], x_refs[i])
    chunks = (count_ref[0] + CHUNK - 1) // CHUNK

    def chunk_step(chunk, _):
        slot = lax.rem(chunk, OUT_RING)

        @pl.when(chunk >= OUT_RING)
        def _():
            out_copy(chunk - OUT_RING).wait()

        def step(k, _):
            j = chunk * CHUNK + SCORE_STEP * k
            for i in range(SCORE_STEP):
                weigh(j + i, s_refs[i], x_refs[i], slot, SCORE_STEP * k + i)
            for i in range(SCORE_STEP):
                score(j + SCORE_STEP + i, s_refs[i], x_refs[i])
            return 0

        lax.fori_loop(0, CHUNK // SCORE_STEP, step, 0)
        out_copy(chunk).start()
        return 0

    lax.fori_loop(0, chunks, chunk_step, 0)
    for back in range(OUT_RING, 0, -1):

        @pl.when(chunks >= back)
        def _():
            out_copy(chunks - back).wait()


def attend_scores(spot, jobs, pieces):
    groups = len(pieces)
    shards, spans, rows, _ = pieces[0].shape
    units = shards * spans
    nblk = units * groups
    room = jobs[1].shape[0] // CHUNK * CHUNK
    work = 3 * units
    return pl.pallas_call(
        functools.partial(scores_kernel, groups),
        in_specs=[SMEM] * 4 + [HBM] * groups,
        out_specs=[HBM, pl.BlockSpec(memory_space=pltpu.VMEM)],
        out_shape=[
            jax.ShapeDtypeStruct((room, BLOCK, rows), BF16),
            jax.ShapeDtypeStruct((room, rows), F32),
        ],
        scratch_shapes=[
            pltpu.VMEM((units, groups, rows, HD), BF16),
            pltpu.VMEM((nblk, BLOCK, HD), F32),
            pltpu.VMEM((8, rows), F32),
            pltpu.VMEM((OUT_RING, CHUNK, BLOCK, rows), BF16),
            pltpu.SemaphoreType.DMA((shards,)),
            pltpu.SemaphoreType.DMA((OUT_RING,)),
            *[pltpu.VMEM((BLOCK, rows), F32)] * SCORE_STEP,
            *[pltpu.VMEM((8, rows), F32)] * SCORE_STEP,
        ],
        cost_estimate=pl.CostEstimate(
            flops=2 * work * rows * BLOCK * HD,
            bytes_accessed=2 * units * groups * rows * HD + 2 * work * rows * BLOCK,
            transcendentals=work * rows * BLOCK,
        ),
        name="attend_scores",
    )(spot, *jobs, *pieces)


def values_kernel(groups, spot_ref, count_ref, unit_ref, key_ref, *refs):
    pieces = refs[:groups]
    p_in, scale_in, o_out, acc_ref, p_buf, o_ref, scale_ref, p_sem, o_sem, scale_sem = refs[groups:]
    units, _, _ = pieces[0].shape
    me = spot_ref[0]
    chunks = (count_ref[0] + CHUNK - 1) // CHUNK

    def in_copy(chunk):
        slot = lax.rem(chunk, IN_RING)
        return pltpu.make_async_copy(
            p_in.at[pl.ds(chunk * CHUNK, CHUNK)], p_buf.at[slot], p_sem.at[slot]
        )

    scale_copy = pltpu.make_async_copy(scale_in, scale_ref, scale_sem)
    scale_copy.start()
    for ahead in range(IN_RING - 1):

        @pl.when(ahead < chunks)
        def _():
            in_copy(ahead).start()

    def clear(unit, _):
        acc_ref[unit] = jnp.zeros(acc_ref.shape[1:], F32)
        return 0

    lax.fori_loop(0, units + 1, clear, 0)
    scale_copy.wait()
    ones = jnp.ones((ONES, BLOCK), BF16)

    def gather(j, prob):
        unit, key = unit_ref[LEAD + j], key_ref[LEAD + j]
        source = lax.rem(key + groups - me, groups)
        turned = pieces[0][key // groups]
        for r in range(1, groups):
            turned = jnp.where(source == r, pieces[r][key // groups], turned)
        part = jnp.dot(
            jnp.concatenate([turned, ones], axis=0), prob, preferred_element_type=F32
        )
        acc_ref[unit] = acc_ref[unit] * scale_ref[pl.ds(j, 1), :] + part[: HD + 8]

    def chunk_step(chunk, _):
        slot = lax.rem(chunk, IN_RING)

        @pl.when(chunk + IN_RING - 1 < chunks)
        def _():
            in_copy(chunk + IN_RING - 1).start()

        in_copy(chunk).wait()

        def step(k, _):
            for i in range(VALUE_STEP):
                at = VALUE_STEP * k + i
                gather(chunk * CHUNK + at, p_buf[slot, at])
            return 0

        lax.fori_loop(0, CHUNK // VALUE_STEP, step, 0)
        return 0

    lax.fori_loop(0, chunks, chunk_step, 0)

    def result(i):
        some = pl.ds(i * FINISH_STEP, FINISH_STEP)
        return pltpu.make_async_copy(o_ref.at[some], o_out.at[some], o_sem.at[i])

    def finish(i, _):
        for k in range(FINISH_STEP):
            unit = i * FINISH_STEP + k
            inverse = 1.0 / acc_ref[unit, HD : HD + 1, :]
            o_ref[unit] = (acc_ref[unit, 0:HD, :] * inverse).astype(BF16).T
        result(i).start()
        return 0

    lax.fori_loop(0, units // FINISH_STEP, finish, 0)
    for i in range(units // FINISH_STEP):
        result(i).wait()


def attend_values(spot, jobs, pieces, probs, scales):
    groups = len(pieces)
    shards, spans, _, rows = pieces[0].shape
    units = shards * spans
    work = 3 * units
    vmem = pl.BlockSpec(memory_space=pltpu.VMEM)
    pieces = [
        pltpu.with_memory_space_constraint(x.reshape(units, HD, rows), pltpu.VMEM)
        for x in pieces
    ]
    return pl.pallas_call(
        functools.partial(values_kernel, groups),
        in_specs=[SMEM] * 4 + [vmem] * groups + [HBM] * 2,
        out_specs=pl.BlockSpec(memory_space=pltpu.HBM),
        out_shape=pltpu.HBM((units, rows, HD), BF16),
        scratch_shapes=[
            pltpu.VMEM((units + 1, HD + 8, rows), F32),
            pltpu.VMEM((IN_RING, CHUNK, BLOCK, rows), BF16),
            pltpu.VMEM((units, rows, HD), BF16),
            pltpu.VMEM(scales.shape, F32),
            pltpu.SemaphoreType.DMA((IN_RING,)),
            pltpu.SemaphoreType.DMA((units // FINISH_STEP,)),
            pltpu.SemaphoreType.DMA,
        ],
        compiler_params=pltpu.CompilerParams(vmem_limit_bytes=24 * MIB),
        cost_estimate=pl.CostEstimate(
            flops=2 * work * rows * BLOCK * HD,
            bytes_accessed=2 * units * groups * rows * HD + 2 * work * rows * BLOCK,
            transcendentals=0,
        ),
        name="attend_values",
    )(spot, *jobs, *pieces, probs, pltpu.with_memory_space_constraint(scales, pltpu.HBM))


def group_shift(x, shards, groups, r):
    pairs = [(i - i % groups + (i % groups + r) % groups, i) for i in range(shards)]
    return lax.ppermute(x, "seq", pairs)


def ring_weights(w_out, groups, member):
    count = lax.axis_size("head")
    here = lax.axis_index("head")
    share = w_out.shape[0] // groups
    up = down = lax.dynamic_slice_in_dim(w_out, member * share, share, 0)
    ups, downs = {}, {}
    for k in range(1, count):
        up = lax.ppermute(up, "head", [(i, i + 1) for i in range(k - 1, count - 1)])
        down = lax.ppermute(down, "head", [(i, i - 1) for i in range(1, count - k + 1)])
        ups[k], downs[k] = up, down
    return [
        jnp.where(here + r < count, downs[r], ups[count - r]) for r in range(1, count)
    ]


def project_kernel(spot_ref, x_ref, w_ref, *refs):
    heads, groups, spans, rows, _ = x_ref.shape
    pieces = refs[: (spans - 1) * groups]
    o_ref, wide_ref, w_buf, sem = refs[(spans - 1) * groups :]
    member, z = spot_ref[0], spot_ref[1]
    tile = w_buf.shape[2]
    share = pieces[0].shape[0]
    depth = heads * HD
    step = pl.program_id(0)

    def copies(slot):
        cols = pl.ds(slot * tile, tile)
        if not isinstance(slot, int):
            cols = pl.ds(pl.multiple_of(slot * tile, tile), tile)
        out = [
            pltpu.make_async_copy(
                w_ref.at[:, cols],
                w_buf.at[slot, pl.ds(pl.multiple_of(z * depth, depth), depth), :],
                sem.at[slot],
            )
        ]
        for r in range(1, spans):
            for k in range(groups):
                at = lax.rem(z + r, spans) * depth + lax.rem(member + k, groups) * share
                out.append(
                    pltpu.make_async_copy(
                        pieces[(r - 1) * groups + k].at[:, cols],
                        w_buf.at[slot, pl.ds(pl.multiple_of(at, share), share), :],
                        sem.at[slot],
                    )
                )
        return out

    @pl.when(step == 0)
    def _():
        for i in range(w_buf.shape[0]):
            for copy in copies(i):
                copy.start()
        for z_at in range(spans):
            for h in range(heads):
                at = (z_at * heads + h) * HD
                for g in range(groups):
                    wide_ref[g * rows : (g + 1) * rows, at : at + HD] = x_ref[h, g, z_at]

    for copy in copies(step):
        copy.wait()
    o_ref[...] = jnp.dot(wide_ref[...], w_buf[step], preferred_element_type=F32).astype(BF16)


def project(spot, mixed, w_out, pieces):
    _, groups, spans, rows, _ = mixed.shape
    depth, width = w_out.shape
    tile = min(PROJECT_TILE, width)
    out_rows = groups * rows
    return pl.pallas_call(
        project_kernel,
        grid=(width // tile,),
        in_specs=[SMEM, pl.BlockSpec(memory_space=pltpu.VMEM)] + [HBM] * (1 + len(pieces)),
        out_specs=pl.BlockSpec((out_rows, tile), lambda i: (0, i)),
        out_shape=jax.ShapeDtypeStruct((out_rows, width), BF16),
        scratch_shapes=[
            pltpu.VMEM((out_rows, spans * depth), BF16),
            pltpu.VMEM((width // tile, spans * depth, tile), BF16),
            pltpu.SemaphoreType.DMA((width // tile,)),
        ],
        cost_estimate=pl.CostEstimate(
            flops=2 * out_rows * spans * depth * width,
            bytes_accessed=2 * spans * depth * width,
            transcendentals=0,
        ),
        name="project",
    )(spot, pltpu.with_memory_space_constraint(mixed, pltpu.VMEM), w_out, *pieces)


def body(qk, values, bucket, pair_row, pair_col, pair_count, w_out):
    shards = lax.axis_size("seq")
    spans = lax.axis_size("head")
    tokens, width = qk.shape
    heads = width // HD
    groups = shards // heads
    blocks = tokens // BLOCK
    slots = pair_row.shape[2]
    here, z = lax.axis_index("seq"), lax.axis_index("head")
    head, member = here // groups, lax.rem(here, groups)
    spot = jnp.stack([member, z, here, z * heads + head]).astype(jnp.int32)

    shares = ring_weights(w_out, groups, member)
    units = shards * spans
    rows = tokens // spans // groups
    turned = rows == BLOCK

    def send(x, turn):
        sent = pack(x, spans, groups, turn)
        sent = sent.reshape(shards, spans, *sent.shape[3:])
        got = lax.all_to_all(sent, "seq", 0, 0, tiled=True)
        return [got] + [group_shift(got, shards, groups, r) for r in range(1, groups)]

    q_pieces = send(qk, False)
    v_pieces = send(values, turned)
    tables = gather_tables(pair_row, pair_col, pair_count, shards)
    jobs = job_lists(
        tables, bucket, spot, shards, slots, blocks, units, tokens // spans, rows
    )
    if turned:
        weights = attend_scores(spot, jobs, q_pieces)
        attn = attend_values(spot, jobs, v_pieces, *weights)
    else:
        attn = attend(spot, jobs, q_pieces, v_pieces)
    mixed = lax.all_to_all(attn, ("seq", "head"), 0, 0, tiled=True)
    mixed = mixed.reshape(heads, groups, spans, rows, HD)
    weights = []
    shares = [pltpu.with_memory_space_constraint(x, pltpu.HBM) for x in shares]
    for piece in shares:
        weights += [piece] + [
            group_shift(piece, shards, groups, k) for k in range(1, groups)
        ]
    weights = [pltpu.with_memory_space_constraint(x, pltpu.HBM) for x in weights]
    return project(spot, mixed, w_out, weights)


def solution(mesh):
    return jax.shard_map(
        body,
        mesh=mesh,
        in_specs=(
            P("seq", "head"),
            P("seq", "head"),
            P(),
            P("seq", None, None),
            P("seq", None, None),
            P("seq", None),
            P("head", None),
        ),
        out_specs=P(("seq", "head"), None),
        check_vma=False,
    )
```

```python
import functools
import math

import jax
import jax.numpy as jnp
from jax import lax
from jax.experimental import pallas as pl
from jax.experimental.pallas import tpu as pltpu
from jax.sharding import PartitionSpec as P


HD = 128
BLOCK = 256
NEG = -1e30
MIB = 1024 * 1024
LEAD, TAIL = 2, 22
PREP_STEP = 4
CHUNK = 8
OUT_RING, IN_RING = 4, 5
SCORE_STEP = 8
VALUE_STEP = 8
ONES = 16
FINISH_STEP = 4
PROJECT_TILE = 512
BF16 = jnp.bfloat16
F32 = jnp.float32
SMEM = pl.BlockSpec(memory_space=pltpu.SMEM)
HBM = pl.BlockSpec(memory_space=pl.ANY)


def turn_kernel(x_ref, o_ref):
    heads, groups = o_ref.shape[:2]
    rows = x_ref.shape[0] // groups
    for h in range(heads):
        for g in range(groups):
            o_ref[h, g, 0] = x_ref[g * rows : (g + 1) * rows, h * HD : (h + 1) * HD].T


def pack_kernel(x_ref, o_ref, held_ref, in_sem, out_sem):
    heads, groups, spans, rows, _ = o_ref.shape
    steps = [(z, g) for z in range(spans) for g in range(groups)]

    def arrive(i):
        some = pl.ds(i * rows, rows)
        return pltpu.make_async_copy(x_ref.at[some], held_ref.at[some], in_sem.at[i])

    def leave(i, h):
        z, g = steps[i]
        return pltpu.make_async_copy(
            held_ref.at[pl.ds(i * rows, rows), pl.ds(h * HD, HD)],
            o_ref.at[h, g, z],
            out_sem.at[i, h],
        )

    for i in range(len(steps)):
        arrive(i).start()
    for i in range(len(steps)):
        arrive(i).wait()
        for h in range(heads):
            leave(i, h).start()
    for i in range(len(steps)):
        for h in range(heads):
            leave(i, h).wait()


def pack(x, spans, groups, turned=False):
    tokens, width = x.shape
    heads, span = width // HD, tokens // spans
    rows = span // groups
    cost = pl.CostEstimate(flops=0, bytes_accessed=4 * tokens * width, transcendentals=0)
    if turned:
        return pl.pallas_call(
            turn_kernel,
            grid=(spans,),
            in_specs=[pl.BlockSpec((span, width), lambda i: (i, 0))],
            out_specs=pl.BlockSpec((heads, groups, 1, HD, rows), lambda i: (0, 0, i, 0, 0)),
            out_shape=jax.ShapeDtypeStruct((heads, groups, spans, HD, rows), BF16),
            cost_estimate=cost,
            name="turn",
        )(x)
    return pl.pallas_call(
        pack_kernel,
        in_specs=[HBM],
        out_specs=HBM,
        out_shape=jax.ShapeDtypeStruct((heads, groups, spans, rows, HD), BF16),
        scratch_shapes=[
            pltpu.VMEM((tokens, width), BF16),
            pltpu.SemaphoreType.DMA((spans * groups,)),
            pltpu.SemaphoreType.DMA((spans * groups, heads)),
        ],
        cost_estimate=cost,
        name="pack",
    )(x)


def gather_tables(pair_row, pair_col, pair_count, shards):
    mine = jnp.concatenate(
        [pair_row.reshape(-1), pair_col.reshape(-1), pair_count.reshape(-1)]
    )
    rest = [
        lax.ppermute(mine, "seq", [((i + r) % shards, i) for i in range(shards)])
        for r in range(1, shards)
    ]
    return jnp.concatenate([mine] + rest)


def job_lists(tables, bucket, spot, shards, slots, blocks, units, span, rows):
    nblk = shards * blocks
    cap = 2 * shards * slots
    limit = job_limit(units, shards, slots)

    def kernel(tab_ref, bucket_ref, spot_ref, count_ref, unit_ref, key_ref, fill, lists):
        head = spot_ref[3]

        def clear(b, _):
            fill[b] = 0
            return 0

        lax.fori_loop(0, nblk, clear, 0)
        per = shards * slots

        for r in range(shards):
            shard = lax.rem(spot_ref[2] + r, shards)
            base = r * (2 * per + shards)

            def to_shard(other, _):
                at = base + other * slots
                live = tab_ref[base + 2 * per + other]
                for slot in range(slots):
                    a = shard * blocks + tab_ref[at + slot]
                    b = other * blocks + tab_ref[at + per + slot]
                    same = bucket_ref[head, a] == bucket_ref[head, b]
                    keep = (same & (slot < live)).astype(jnp.int32)
                    end_a, end_b = fill[a], fill[b]
                    lists[a * (cap + 1) + end_a] = b
                    lists[b * (cap + 1) + end_b] = a
                    fill[a] = end_a + keep
                    fill[b] = end_b + keep
                return 0

            lax.fori_loop(0, shards, to_shard, 0, unroll=4)

        for i in range(LEAD):
            unit_ref[i] = units
            key_ref[i] = 0

        def per_unit(unit, at):
            own = (unit * span + spot_ref[0] * rows) // BLOCK
            unit_ref[at] = unit
            key_ref[at] = own
            n = fill[own]

            def partner(j, _):
                unit_ref[at + 1 + j] = unit
                key_ref[at + 1 + j] = lists[own * (cap + 1) + j]
                return 0

            lax.fori_loop(0, n, partner, 0)
            return at + 1 + n

        end = lax.fori_loop(0, units, per_unit, LEAD)
        for i in range(TAIL):
            unit_ref[end + i] = units
            key_ref[end + i] = 0
        count_ref[0] = end - LEAD

    return pl.pallas_call(
        kernel,
        in_specs=[SMEM] * 3,
        out_specs=[SMEM, SMEM, SMEM],
        out_shape=[
            jax.ShapeDtypeStruct((1,), jnp.int32),
            jax.ShapeDtypeStruct((limit,), jnp.int32),
            jax.ShapeDtypeStruct((limit,), jnp.int32),
        ],
        scratch_shapes=[
            pltpu.SMEM((nblk,), jnp.int32),
            pltpu.SMEM((nblk * (cap + 1),), jnp.int32),
        ],
        cost_estimate=pl.CostEstimate(
            flops=0, bytes_accessed=32 * 1024 * 1024, transcendentals=0
        ),
        name="job_lists",
    )(tables, bucket.T, spot)


def job_limit(units, shards, slots):
    return units + 2 * shards * shards * slots + LEAD + TAIL


def attend_kernel(groups, spot_ref, count_ref, unit_ref, key_ref, *refs):
    pieces = refs[:groups], refs[groups : 2 * groups]
    refs = refs[groups:]
    o_ref, q_ref, v_ref, vt_ref, inv_ref, s0, s1, x0, x1, p0, p1, a0, a1 = refs[
        groups : groups + 13
    ]
    top_ref, sum_ref, acc_ref, q_sem, v_sem = refs[groups + 13 :]
    units, span, _ = q_ref.shape
    rows = span // groups
    spans = pieces[0][0].shape[1]
    shards = units // spans
    blocks_per = span // BLOCK
    me = spot_ref[0]
    lanes = [slice(k, min(k + HD, rows)) for k in range(0, rows, HD)]

    copies = ([], [])
    for r in range(groups):
        piece = lax.rem(me + r, groups)
        for part, ref, sem in ((0, q_ref, q_sem), (1, v_ref, v_sem)):
            for s in range(shards):
                copies[part].append(
                    pltpu.make_async_copy(
                        pieces[part][r].at[s],
                        ref.at[pl.ds(s * spans, spans), pl.ds(piece * rows, rows), :],
                        sem,
                    )
                )
    for part in copies:
        for copy in part:
            copy.start()

    def clear(unit, _):
        sum_ref[unit] = jnp.zeros(sum_ref.shape[1:], F32)
        acc_ref[unit] = jnp.zeros(acc_ref.shape[1:], F32)
        return 0

    lax.fori_loop(0, units + 1, clear, 0)
    for part in copies:
        for copy in part:
            copy.wait()

    def block_at(b):
        if blocks_per == 1:
            return b, slice(None)
        unit = b // blocks_per
        return unit, pl.ds(pl.multiple_of((b - unit * blocks_per) * BLOCK, BLOCK), BLOCK)

    ones = jnp.ones((HD, HD), BF16)
    contract = (((1,), (1,)), ((), ()))

    def prepare(i, _):
        for k in range(PREP_STEP):
            b = i * PREP_STEP + k
            unit, at = block_at(b)
            wide = q_ref[unit, at, :].astype(F32)
            square = wide * wide
            high = square.astype(BF16)
            low = (square - high.astype(F32)).astype(BF16)
            total = jnp.dot(high, ones, preferred_element_type=F32)
            total += jnp.dot(low, ones, preferred_element_type=F32)
            scale = math.log2(math.e) / math.sqrt(HD)
            inv_ref[b] = lax.rsqrt(total * (1.0 / HD) + 1e-06) * scale
            vt_ref[b] = v_ref[unit, at, :].T
        return 0

    lax.fori_loop(0, units * blocks_per // PREP_STEP, prepare, 0)

    def tiles(x):
        return x.reshape(x.shape[0] // 8, 8, x.shape[1])

    def score(t, s_ref, x_ref):
        unit, key = jnp.minimum(unit_ref[t], units - 1), key_ref[t]
        first = unit_ref[t - 1] != unit_ref[t]
        query = q_ref[unit, pl.ds(pl.multiple_of(me * rows, rows), rows), :]
        u, at = block_at(key)
        gram = lax.dot_general(q_ref[u, at, :], query, contract, preferred_element_type=F32)
        offset = lax.rem(unit * span + me * rows, BLOCK)
        shift = jnp.where(first, offset, 2 * BLOCK)
        for lane in lanes:
            n = lane.stop - lane.start
            part = gram[:, lane] * inv_ref[key, :, 0:n]
            lo, hi = (lane.start, lane.stop) if rows == BLOCK else (0, BLOCK)
            band = part[lo:hi]
            row = lax.broadcasted_iota(jnp.int32, band.shape, 0) + (lo - lane.start)
            col = lax.broadcasted_iota(jnp.int32, band.shape, 1)
            band = jnp.where(row - col == shift, NEG, band)
            above = [part[:lo]] if lo else []
            below = [part[hi:]] if hi < BLOCK else []
            part = jnp.concatenate(above + [band] + below, axis=0)
            s_ref[:, lane] = part
            most = jnp.max(jnp.max(tiles(part), axis=0), axis=0, keepdims=True)
            x_ref[:, lane] = jnp.broadcast_to(most, (8, n))

    def weigh(t, s_ref, x_ref, p_ref, a_ref):
        unit = unit_ref[t]
        first = unit_ref[t - 1] != unit
        old = jnp.where(first, 2 * NEG, top_ref[...])
        new = jnp.maximum(old, x_ref[...])
        top_ref[...] = new
        scale = jnp.exp2(old - new)
        a_ref[...] = scale
        for lane in lanes:
            prob = jnp.exp2(tiles(s_ref[:, lane]) - new[None, :, lane])
            sum_ref[unit, :, lane] = sum_ref[unit, :, lane] * scale[:, lane] + jnp.sum(
                prob, axis=0
            )
            p_ref[:, lane] = prob.reshape(BLOCK, lane.stop - lane.start).astype(BF16)

    def gather(t, p_ref, a_ref):
        unit, key = unit_ref[t], key_ref[t]
        part = jnp.dot(vt_ref[key], p_ref[...], preferred_element_type=F32)
        kept = tiles(acc_ref[unit]) * a_ref[...][None]
        acc_ref[unit] = kept.reshape(HD, rows) + part

    def pair_step(i, _):
        t = LEAD + 2 * i
        gather(t - 2, p0, a0)
        weigh(t - 1, s1, x1, p1, a1)
        score(t, s0, x0)
        gather(t - 1, p1, a1)
        weigh(t, s0, x0, p0, a0)
        score(t + 1, s1, x1)
        return 0

    lax.fori_loop(0, (count_ref[0] + 1) // 2 + 1, pair_step, 0)

    def finish(unit, _):
        total = 1.0 / jnp.sum(sum_ref[unit], axis=0, keepdims=True)
        o_ref[unit] = (acc_ref[unit] * total).T.astype(BF16)
        return 0

    lax.fori_loop(0, units, finish, 0)


def attend(spot, jobs, q_pieces, v_pieces):
    groups = len(q_pieces)
    shards, spans, rows, _ = q_pieces[0].shape
    units, span = shards * spans, rows * groups
    nblk = units * span // BLOCK
    work = 3 * units
    scores = pltpu.VMEM((BLOCK, rows), F32)
    probs = pltpu.VMEM((BLOCK, rows), BF16)
    line = pltpu.VMEM((8, rows), F32)
    return pl.pallas_call(
        functools.partial(attend_kernel, groups),
        in_specs=[SMEM] * 4 + [HBM] * (2 * groups),
        out_specs=pl.BlockSpec(memory_space=pltpu.VMEM),
        out_shape=jax.ShapeDtypeStruct((units, rows, HD), BF16),
        scratch_shapes=[
            pltpu.VMEM((units, span, HD), BF16),
            pltpu.VMEM((units, span, HD), BF16),
            pltpu.VMEM((nblk, HD, BLOCK), BF16),
            pltpu.VMEM((nblk, BLOCK, HD), F32),
            *[scores, scores, line, line, probs, probs, line, line],
            line,
            pltpu.VMEM((units + 1, 8, rows), F32),
            pltpu.VMEM((units + 1, HD, rows), F32),
            pltpu.SemaphoreType.DMA,
            pltpu.SemaphoreType.DMA,
        ],
        cost_estimate=pl.CostEstimate(
            flops=4 * work * rows * BLOCK * HD,
            bytes_accessed=4 * units * span * HD,
            transcendentals=work * rows * BLOCK,
        ),
        name="attend",
    )(spot, *jobs, *q_pieces, *v_pieces)


def scores_kernel(groups, spot_ref, count_ref, unit_ref, key_ref, *refs):
    pieces = refs[:groups]
    p_out, scale_ref, q_ref, inv_ref, top_ref, p_buf, q_sem, p_sem = refs[groups : groups + 8]
    held = refs[groups + 8 :]
    s_refs, x_refs = held[:SCORE_STEP], held[SCORE_STEP:]
    shards, spans, rows, _ = pieces[0].shape
    units = shards * spans
    me = spot_ref[0]
    lanes = [slice(k, k + HD) for k in range(0, rows, HD)]

    def arrivals(s):
        some = pl.ds(s * spans, spans)
        return [
            pltpu.make_async_copy(
                pieces[r].at[s], q_ref.at[some, lax.rem(me + r, groups)], q_sem.at[s]
            )
            for r in range(groups)
        ]

    for s in range(shards):
        for copy in arrivals(s):
            copy.start()

    fold = math.log2(math.e) ** -2

    def prepare(s, _):
        for copy in arrivals(s):
            copy.wait()
        for k in range(spans * groups):
            unit, piece = s * spans + k // groups, k % groups
            wide = q_ref[unit, piece].astype(F32)
            total = jnp.sum(wide * wide, axis=1, keepdims=True)
            inv = lax.rsqrt(total * fold + 1e-06 * HD * fold)
            inv_ref[unit * groups + piece] = jnp.broadcast_to(inv, (BLOCK, HD))
        return 0

    lax.fori_loop(0, shards, prepare, 0)

    def tiles(x):
        return x.reshape(x.shape[0] // 8, 8, x.shape[1])

    def score(j, s_ref, x_ref):
        t = LEAD + j
        unit, key = jnp.minimum(unit_ref[t], units - 1), key_ref[t]
        first = unit_ref[t - 1] != unit_ref[t]
        gram = lax.dot_general(
            q_ref[key // groups, lax.rem(key, groups)],
            q_ref[unit, me],
            (((1,), (1,)), ((), ())),
            preferred_element_type=F32,
        )
        shift = jnp.where(first, 0, 2 * BLOCK)
        for lane in lanes:
            part = gram[:, lane] * inv_ref[key]
            band = part[lane]
            row = lax.broadcasted_iota(jnp.int32, band.shape, 0)
            col = lax.broadcasted_iota(jnp.int32, band.shape, 1)
            band = jnp.where(row - col == shift, NEG, band)
            above = [part[: lane.start]] if lane.start else []
            below = [part[lane.stop :]] if lane.stop < BLOCK else []
            part = jnp.concatenate(above + [band] + below, axis=0)
            s_ref[:, lane] = part
            most = jnp.max(jnp.max(tiles(part), axis=0), axis=0, keepdims=True)
            x_ref[:, lane] = jnp.broadcast_to(most, (8, HD))

    def weigh(j, s_ref, x_ref, slot, at):
        first = unit_ref[LEAD + j - 1] != unit_ref[LEAD + j]
        old = jnp.where(first, 2 * NEG, top_ref[...])
        new = jnp.maximum(old, x_ref[...])
        top_ref[...] = new
        scale_ref[pl.ds(j, 1), :] = jnp.exp2(old - new)[0:1]
        for lane in lanes:
            prob = jnp.exp2(tiles(s_ref[:, lane]) - new[None, :, lane])
            p_buf[slot, at, :, lane] = prob.reshape(BLOCK, HD).astype(BF16)

    def out_copy(chunk):
        slot = lax.rem(chunk, OUT_RING)
        return pltpu.make_async_copy(
            p_buf.at[slot], p_out.at[pl.ds(chunk * CHUNK, CHUNK)], p_sem.at[slot]
        )

    for i in range(SCORE_STEP):
        score(i, s_refs[i], x_refs[i])
    chunks = (count_ref[0] + CHUNK - 1) // CHUNK

    def chunk_step(chunk, _):
        slot = lax.rem(chunk, OUT_RING)

        @pl.when(chunk >= OUT_RING)
        def _():
            out_copy(chunk - OUT_RING).wait()

        def step(k, _):
            j = chunk * CHUNK + SCORE_STEP * k
            for i in range(SCORE_STEP):
                weigh(j + i, s_refs[i], x_refs[i], slot, SCORE_STEP * k + i)
            for i in range(SCORE_STEP):
                score(j + SCORE_STEP + i, s_refs[i], x_refs[i])
            return 0

        lax.fori_loop(0, CHUNK // SCORE_STEP, step, 0)
        out_copy(chunk).start()
        return 0

    lax.fori_loop(0, chunks, chunk_step, 0)
    for back in range(OUT_RING, 0, -1):

        @pl.when(chunks >= back)
        def _():
            out_copy(chunks - back).wait()


def attend_scores(spot, jobs, pieces):
    groups = len(pieces)
    shards, spans, rows, _ = pieces[0].shape
    units = shards * spans
    nblk = units * groups
    room = jobs[1].shape[0] // CHUNK * CHUNK
    work = 3 * units
    return pl.pallas_call(
        functools.partial(scores_kernel, groups),
        in_specs=[SMEM] * 4 + [HBM] * groups,
        out_specs=[HBM, pl.BlockSpec(memory_space=pltpu.VMEM)],
        out_shape=[
            jax.ShapeDtypeStruct((room, BLOCK, rows), BF16),
            jax.ShapeDtypeStruct((room, rows), F32),
        ],
        scratch_shapes=[
            pltpu.VMEM((units, groups, rows, HD), BF16),
            pltpu.VMEM((nblk, BLOCK, HD), F32),
            pltpu.VMEM((8, rows), F32),
            pltpu.VMEM((OUT_RING, CHUNK, BLOCK, rows), BF16),
            pltpu.SemaphoreType.DMA((shards,)),
            pltpu.SemaphoreType.DMA((OUT_RING,)),
            *[pltpu.VMEM((BLOCK, rows), F32)] * SCORE_STEP,
            *[pltpu.VMEM((8, rows), F32)] * SCORE_STEP,
        ],
        cost_estimate=pl.CostEstimate(
            flops=2 * work * rows * BLOCK * HD,
            bytes_accessed=2 * units * groups * rows * HD + 2 * work * rows * BLOCK,
            transcendentals=work * rows * BLOCK,
        ),
        name="attend_scores",
    )(spot, *jobs, *pieces)


def values_kernel(groups, spot_ref, count_ref, unit_ref, key_ref, *refs):
    pieces = refs[:groups]
    p_in, scale_in, o_out, acc_ref, p_buf, o_ref, scale_ref, p_sem, o_sem, scale_sem = refs[groups:]
    units, _, _ = pieces[0].shape
    me = spot_ref[0]
    chunks = (count_ref[0] + CHUNK - 1) // CHUNK

    def in_copy(chunk):
        slot = lax.rem(chunk, IN_RING)
        return pltpu.make_async_copy(
            p_in.at[pl.ds(chunk * CHUNK, CHUNK)], p_buf.at[slot], p_sem.at[slot]
        )

    scale_copy = pltpu.make_async_copy(scale_in, scale_ref, scale_sem)
    scale_copy.start()
    for ahead in range(IN_RING - 1):

        @pl.when(ahead < chunks)
        def _():
            in_copy(ahead).start()

    def clear(unit, _):
        acc_ref[unit] = jnp.zeros(acc_ref.shape[1:], F32)
        return 0

    lax.fori_loop(0, units + 1, clear, 0)
    scale_copy.wait()
    ones = jnp.ones((ONES, BLOCK), BF16)

    def gather(j, prob):
        unit, key = unit_ref[LEAD + j], key_ref[LEAD + j]
        source = lax.rem(key + groups - me, groups)
        turned = pieces[0][key // groups]
        for r in range(1, groups):
            turned = jnp.where(source == r, pieces[r][key // groups], turned)
        part = jnp.dot(
            jnp.concatenate([turned, ones], axis=0), prob, preferred_element_type=F32
        )
        acc_ref[unit] = acc_ref[unit] * scale_ref[pl.ds(j, 1), :] + part[: HD + 8]

    def chunk_step(chunk, _):
        slot = lax.rem(chunk, IN_RING)

        @pl.when(chunk + IN_RING - 1 < chunks)
        def _():
            in_copy(chunk + IN_RING - 1).start()

        in_copy(chunk).wait()

        def step(k, _):
            for i in range(VALUE_STEP):
                at = VALUE_STEP * k + i
                gather(chunk * CHUNK + at, p_buf[slot, at])
            return 0

        lax.fori_loop(0, CHUNK // VALUE_STEP, step, 0)
        return 0

    lax.fori_loop(0, chunks, chunk_step, 0)

    def result(i):
        some = pl.ds(i * FINISH_STEP, FINISH_STEP)
        return pltpu.make_async_copy(o_ref.at[some], o_out.at[some], o_sem.at[i])

    def finish(i, _):
        for k in range(FINISH_STEP):
            unit = i * FINISH_STEP + k
            inverse = 1.0 / acc_ref[unit, HD : HD + 1, :]
            o_ref[unit] = (acc_ref[unit, 0:HD, :] * inverse).astype(BF16).T
        result(i).start()
        return 0

    lax.fori_loop(0, units // FINISH_STEP, finish, 0)
    for i in range(units // FINISH_STEP):
        result(i).wait()


def attend_values(spot, jobs, pieces, probs, scales):
    groups = len(pieces)
    shards, spans, _, rows = pieces[0].shape
    units = shards * spans
    work = 3 * units
    vmem = pl.BlockSpec(memory_space=pltpu.VMEM)
    pieces = [
        pltpu.with_memory_space_constraint(x.reshape(units, HD, rows), pltpu.VMEM)
        for x in pieces
    ]
    return pl.pallas_call(
        functools.partial(values_kernel, groups),
        in_specs=[SMEM] * 4 + [vmem] * groups + [HBM] * 2,
        out_specs=pl.BlockSpec(memory_space=pltpu.HBM),
        out_shape=pltpu.HBM((units, rows, HD), BF16),
        scratch_shapes=[
            pltpu.VMEM((units + 1, HD + 8, rows), F32),
            pltpu.VMEM((IN_RING, CHUNK, BLOCK, rows), BF16),
            pltpu.VMEM((units, rows, HD), BF16),
            pltpu.VMEM(scales.shape, F32),
            pltpu.SemaphoreType.DMA((IN_RING,)),
            pltpu.SemaphoreType.DMA((units // FINISH_STEP,)),
            pltpu.SemaphoreType.DMA,
        ],
        compiler_params=pltpu.CompilerParams(vmem_limit_bytes=24 * MIB),
        cost_estimate=pl.CostEstimate(
            flops=2 * work * rows * BLOCK * HD,
            bytes_accessed=2 * units * groups * rows * HD + 2 * work * rows * BLOCK,
            transcendentals=0,
        ),
        name="attend_values",
    )(spot, *jobs, *pieces, probs, pltpu.with_memory_space_constraint(scales, pltpu.HBM))


def group_shift(x, shards, groups, r):
    pairs = [(i - i % groups + (i % groups + r) % groups, i) for i in range(shards)]
    return lax.ppermute(x, "seq", pairs)


def ring_weights(w_out, groups, member):
    count = lax.axis_size("head")
    here = lax.axis_index("head")
    share = w_out.shape[0] // groups
    up = down = lax.dynamic_slice_in_dim(w_out, member * share, share, 0)
    ups, downs = {}, {}
    for k in range(1, count):
        up = lax.ppermute(up, "head", [(i, i + 1) for i in range(k - 1, count - 1)])
        down = lax.ppermute(down, "head", [(i, i - 1) for i in range(1, count - k + 1)])
        ups[k], downs[k] = up, down
    return [
        jnp.where(here + r < count, downs[r], ups[count - r]) for r in range(1, count)
    ]


def project_kernel(spot_ref, x_ref, w_ref, *refs):
    heads, groups, spans, rows, _ = x_ref.shape
    pieces = refs[: (spans - 1) * groups]
    o_ref, wide_ref, w_buf, sem = refs[(spans - 1) * groups :]
    member, z = spot_ref[0], spot_ref[1]
    tile = w_buf.shape[2]
    share = pieces[0].shape[0]
    depth = heads * HD
    step = pl.program_id(0)

    def copies(slot):
        cols = pl.ds(slot * tile, tile)
        if not isinstance(slot, int):
            cols = pl.ds(pl.multiple_of(slot * tile, tile), tile)
        out = [
            pltpu.make_async_copy(
                w_ref.at[:, cols],
                w_buf.at[slot, pl.ds(pl.multiple_of(z * depth, depth), depth), :],
                sem.at[slot],
            )
        ]
        for r in range(1, spans):
            for k in range(groups):
                at = lax.rem(z + r, spans) * depth + lax.rem(member + k, groups) * share
                out.append(
                    pltpu.make_async_copy(
                        pieces[(r - 1) * groups + k].at[:, cols],
                        w_buf.at[slot, pl.ds(pl.multiple_of(at, share), share), :],
                        sem.at[slot],
                    )
                )
        return out

    @pl.when(step == 0)
    def _():
        for i in range(w_buf.shape[0]):
            for copy in copies(i):
                copy.start()
        for z_at in range(spans):
            for h in range(heads):
                at = (z_at * heads + h) * HD
                for g in range(groups):
                    wide_ref[g * rows : (g + 1) * rows, at : at + HD] = x_ref[h, g, z_at]

    for copy in copies(step):
        copy.wait()
    o_ref[...] = jnp.dot(wide_ref[...], w_buf[step], preferred_element_type=F32).astype(BF16)


def project(spot, mixed, w_out, pieces):
    _, groups, spans, rows, _ = mixed.shape
    depth, width = w_out.shape
    tile = min(PROJECT_TILE, width)
    out_rows = groups * rows
    return pl.pallas_call(
        project_kernel,
        grid=(width // tile,),
        in_specs=[SMEM, pl.BlockSpec(memory_space=pltpu.VMEM)] + [HBM] * (1 + len(pieces)),
        out_specs=pl.BlockSpec((out_rows, tile), lambda i: (0, i)),
        out_shape=jax.ShapeDtypeStruct((out_rows, width), BF16),
        scratch_shapes=[
            pltpu.VMEM((out_rows, spans * depth), BF16),
            pltpu.VMEM((width // tile, spans * depth, tile), BF16),
            pltpu.SemaphoreType.DMA((width // tile,)),
        ],
        cost_estimate=pl.CostEstimate(
            flops=2 * out_rows * spans * depth * width,
            bytes_accessed=2 * spans * depth * width,
            transcendentals=0,
        ),
        name="project",
    )(spot, pltpu.with_memory_space_constraint(mixed, pltpu.VMEM), w_out, *pieces)


def body(qk, values, bucket, pair_row, pair_col, pair_count, w_out):
    shards = lax.axis_size("seq")
    spans = lax.axis_size("head")
    tokens, width = qk.shape
    heads = width // HD
    groups = shards // heads
    blocks = tokens // BLOCK
    slots = pair_row.shape[2]
    here, z = lax.axis_index("seq"), lax.axis_index("head")
    head, member = here // groups, lax.rem(here, groups)
    spot = jnp.stack([member, z, here, z * heads + head]).astype(jnp.int32)

    shares = ring_weights(w_out, groups, member)
    units = shards * spans
    rows = tokens // spans // groups
    turned = rows == BLOCK

    def send(x, turn):
        sent = pack(x, spans, groups, turn)
        sent = sent.reshape(shards, spans, *sent.shape[3:])
        got = lax.all_to_all(sent, "seq", 0, 0, tiled=True)
        return [got] + [group_shift(got, shards, groups, r) for r in range(1, groups)]

    q_pieces = send(qk, False)
    v_pieces = send(values, turned)
    tables = gather_tables(pair_row, pair_col, pair_count, shards)
    jobs = job_lists(
        tables, bucket, spot, shards, slots, blocks, units, tokens // spans, rows
    )
    if turned:
        weights = attend_scores(spot, jobs, q_pieces)
        attn = attend_values(spot, jobs, v_pieces, *weights)
    else:
        attn = attend(spot, jobs, q_pieces, v_pieces)
    mixed = lax.all_to_all(attn, ("seq", "head"), 0, 0, tiled=True)
    mixed = mixed.reshape(heads, groups, spans, rows, HD)
    weights = []
    shares = [pltpu.with_memory_space_constraint(x, pltpu.HBM) for x in shares]
    for piece in shares:
        weights += [piece] + [
            group_shift(piece, shards, groups, k) for k in range(1, groups)
        ]
    weights = [pltpu.with_memory_space_constraint(x, pltpu.HBM) for x in weights]
    return project(spot, mixed, w_out, weights)


def solution(mesh):
    return jax.shard_map(
        body,
        mesh=mesh,
        in_specs=(
            P("seq", "head"),
            P("seq", "head"),
            P(),
            P("seq", None, None),
            P("seq", None, None),
            P("seq", None),
            P("head", None),
        ),
        out_specs=P(("seq", "head"), None),
        check_vma=False,
    )
```

```python
import functools
import math

import jax
import jax.numpy as jnp
from jax import lax
from jax.experimental import pallas as pl
from jax.experimental.pallas import tpu as pltpu
from jax.sharding import PartitionSpec as P


HD = 128
BLOCK = 256
NEG = -1e30
MIB = 1024 * 1024
LEAD, TAIL = 2, 30
PREP_STEP = 4
CHUNK = 16
OUT_RING, IN_RING = 3, 3
SCORE_STEP = 8
VALUE_STEP = 16
ONES = 16
FINISH_STEP = 4
PROJECT_TILE = 512
BF16 = jnp.bfloat16
F32 = jnp.float32
SMEM = pl.BlockSpec(memory_space=pltpu.SMEM)
HBM = pl.BlockSpec(memory_space=pl.ANY)


def turn_kernel(x_ref, o_ref):
    heads, groups = o_ref.shape[:2]
    rows = x_ref.shape[0] // groups
    for h in range(heads):
        for g in range(groups):
            o_ref[h, g, 0] = x_ref[g * rows : (g + 1) * rows, h * HD : (h + 1) * HD].T


def pack_kernel(x_ref, o_ref, held_ref, in_sem, out_sem):
    heads, groups, spans, rows, _ = o_ref.shape
    steps = [(z, g) for z in range(spans) for g in range(groups)]

    def arrive(i):
        some = pl.ds(i * rows, rows)
        return pltpu.make_async_copy(x_ref.at[some], held_ref.at[some], in_sem.at[i])

    def leave(i, h):
        z, g = steps[i]
        return pltpu.make_async_copy(
            held_ref.at[pl.ds(i * rows, rows), pl.ds(h * HD, HD)],
            o_ref.at[h, g, z],
            out_sem.at[i, h],
        )

    for i in range(len(steps)):
        arrive(i).start()
    for i in range(len(steps)):
        arrive(i).wait()
        for h in range(heads):
            leave(i, h).start()
    for i in range(len(steps)):
        for h in range(heads):
            leave(i, h).wait()


def pack(x, spans, groups, turned=False):
    tokens, width = x.shape
    heads, span = width // HD, tokens // spans
    rows = span // groups
    cost = pl.CostEstimate(flops=0, bytes_accessed=4 * tokens * width, transcendentals=0)
    if turned:
        return pl.pallas_call(
            turn_kernel,
            grid=(spans,),
            in_specs=[pl.BlockSpec((span, width), lambda i: (i, 0))],
            out_specs=pl.BlockSpec((heads, groups, 1, HD, rows), lambda i: (0, 0, i, 0, 0)),
            out_shape=jax.ShapeDtypeStruct((heads, groups, spans, HD, rows), BF16),
            cost_estimate=cost,
            name="turn",
        )(x)
    return pl.pallas_call(
        pack_kernel,
        in_specs=[HBM],
        out_specs=HBM,
        out_shape=jax.ShapeDtypeStruct((heads, groups, spans, rows, HD), BF16),
        scratch_shapes=[
            pltpu.VMEM((tokens, width), BF16),
            pltpu.SemaphoreType.DMA((spans * groups,)),
            pltpu.SemaphoreType.DMA((spans * groups, heads)),
        ],
        cost_estimate=cost,
        name="pack",
    )(x)


def gather_tables(pair_row, pair_col, pair_count, shards):
    mine = jnp.concatenate(
        [pair_row.reshape(-1), pair_col.reshape(-1), pair_count.reshape(-1)]
    )
    rest = [
        lax.ppermute(mine, "seq", [((i + r) % shards, i) for i in range(shards)])
        for r in range(1, shards)
    ]
    return jnp.concatenate([mine] + rest)


def job_lists(tables, bucket, spot, shards, slots, blocks, units, span, rows):
    nblk = shards * blocks
    cap = 2 * shards * slots
    limit = job_limit(units, shards, slots)

    def kernel(tab_ref, bucket_ref, spot_ref, count_ref, unit_ref, key_ref, fill, lists):
        head = spot_ref[3]

        def clear(b, _):
            fill[b] = 0
            return 0

        lax.fori_loop(0, nblk, clear, 0)
        per = shards * slots

        for r in range(shards):
            shard = lax.rem(spot_ref[2] + r, shards)
            base = r * (2 * per + shards)

            def to_shard(other, _):
                at = base + other * slots
                live = tab_ref[base + 2 * per + other]
                for slot in range(slots):
                    a = shard * blocks + tab_ref[at + slot]
                    b = other * blocks + tab_ref[at + per + slot]
                    same = bucket_ref[head, a] == bucket_ref[head, b]
                    keep = (same & (slot < live)).astype(jnp.int32)
                    end_a, end_b = fill[a], fill[b]
                    lists[a * (cap + 1) + end_a] = b
                    lists[b * (cap + 1) + end_b] = a
                    fill[a] = end_a + keep
                    fill[b] = end_b + keep
                return 0

            lax.fori_loop(0, shards, to_shard, 0)

        for i in range(LEAD):
            unit_ref[i] = units
            key_ref[i] = 0

        def per_unit(unit, at):
            own = (unit * span + spot_ref[0] * rows) // BLOCK
            unit_ref[at] = unit
            key_ref[at] = own
            n = fill[own]

            def partner(j, _):
                unit_ref[at + 1 + j] = unit
                key_ref[at + 1 + j] = lists[own * (cap + 1) + j]
                return 0

            lax.fori_loop(0, n, partner, 0)
            return at + 1 + n

        end = lax.fori_loop(0, units, per_unit, LEAD)
        for i in range(TAIL):
            unit_ref[end + i] = units
            key_ref[end + i] = 0
        count_ref[0] = end - LEAD

    return pl.pallas_call(
        kernel,
        in_specs=[SMEM] * 3,
        out_specs=[SMEM, SMEM, SMEM],
        out_shape=[
            jax.ShapeDtypeStruct((1,), jnp.int32),
            jax.ShapeDtypeStruct((limit,), jnp.int32),
            jax.ShapeDtypeStruct((limit,), jnp.int32),
        ],
        scratch_shapes=[
            pltpu.SMEM((nblk,), jnp.int32),
            pltpu.SMEM((nblk * (cap + 1),), jnp.int32),
        ],
        cost_estimate=pl.CostEstimate(
            flops=0, bytes_accessed=32 * 1024 * 1024, transcendentals=0
        ),
        name="job_lists",
    )(tables, bucket.T, spot)


def job_limit(units, shards, slots):
    return units + 2 * shards * shards * slots + LEAD + TAIL


def attend_kernel(groups, spot_ref, count_ref, unit_ref, key_ref, *refs):
    pieces = refs[:groups], refs[groups : 2 * groups]
    refs = refs[groups:]
    o_ref, q_ref, v_ref, vt_ref, inv_ref, s0, s1, x0, x1, p0, p1, a0, a1 = refs[
        groups : groups + 13
    ]
    top_ref, sum_ref, acc_ref, q_sem, v_sem = refs[groups + 13 :]
    units, span, _ = q_ref.shape
    rows = span // groups
    spans = pieces[0][0].shape[1]
    shards = units // spans
    blocks_per = span // BLOCK
    me = spot_ref[0]
    lanes = [slice(k, min(k + HD, rows)) for k in range(0, rows, HD)]

    copies = ([], [])
    for r in range(groups):
        piece = lax.rem(me + r, groups)
        for part, ref, sem in ((0, q_ref, q_sem), (1, v_ref, v_sem)):
            for s in range(shards):
                copies[part].append(
                    pltpu.make_async_copy(
                        pieces[part][r].at[s],
                        ref.at[pl.ds(s * spans, spans), pl.ds(piece * rows, rows), :],
                        sem,
                    )
                )
    for part in copies:
        for copy in part:
            copy.start()

    def clear(unit, _):
        sum_ref[unit] = jnp.zeros(sum_ref.shape[1:], F32)
        acc_ref[unit] = jnp.zeros(acc_ref.shape[1:], F32)
        return 0

    lax.fori_loop(0, units + 1, clear, 0)
    for part in copies:
        for copy in part:
            copy.wait()

    def block_at(b):
        if blocks_per == 1:
            return b, slice(None)
        unit = b // blocks_per
        return unit, pl.ds(pl.multiple_of((b - unit * blocks_per) * BLOCK, BLOCK), BLOCK)

    ones = jnp.ones((HD, HD), BF16)
    contract = (((1,), (1,)), ((), ()))

    def prepare(i, _):
        for k in range(PREP_STEP):
            b = i * PREP_STEP + k
            unit, at = block_at(b)
            wide = q_ref[unit, at, :].astype(F32)
            square = wide * wide
            high = square.astype(BF16)
            low = (square - high.astype(F32)).astype(BF16)
            total = jnp.dot(high, ones, preferred_element_type=F32)
            total += jnp.dot(low, ones, preferred_element_type=F32)
            scale = math.log2(math.e) / math.sqrt(HD)
            inv_ref[b] = lax.rsqrt(total * (1.0 / HD) + 1e-06) * scale
            vt_ref[b] = v_ref[unit, at, :].T
        return 0

    lax.fori_loop(0, units * blocks_per // PREP_STEP, prepare, 0)

    def tiles(x):
        return x.reshape(x.shape[0] // 8, 8, x.shape[1])

    def score(t, s_ref, x_ref):
        unit, key = jnp.minimum(unit_ref[t], units - 1), key_ref[t]
        first = unit_ref[t - 1] != unit_ref[t]
        query = q_ref[unit, pl.ds(pl.multiple_of(me * rows, rows), rows), :]
        u, at = block_at(key)
        gram = lax.dot_general(q_ref[u, at, :], query, contract, preferred_element_type=F32)
        offset = lax.rem(unit * span + me * rows, BLOCK)
        shift = jnp.where(first, offset, 2 * BLOCK)
        for lane in lanes:
            n = lane.stop - lane.start
            part = gram[:, lane] * inv_ref[key, :, 0:n]
            lo, hi = (lane.start, lane.stop) if rows == BLOCK else (0, BLOCK)
            band = part[lo:hi]
            row = lax.broadcasted_iota(jnp.int32, band.shape, 0) + (lo - lane.start)
            col = lax.broadcasted_iota(jnp.int32, band.shape, 1)
            band = jnp.where(row - col == shift, NEG, band)
            above = [part[:lo]] if lo else []
            below = [part[hi:]] if hi < BLOCK else []
            part = jnp.concatenate(above + [band] + below, axis=0)
            s_ref[:, lane] = part
            most = jnp.max(jnp.max(tiles(part), axis=0), axis=0, keepdims=True)
            x_ref[:, lane] = jnp.broadcast_to(most, (8, n))

    def weigh(t, s_ref, x_ref, p_ref, a_ref):
        unit = unit_ref[t]
        first = unit_ref[t - 1] != unit
        old = jnp.where(first, 2 * NEG, top_ref[...])
        new = jnp.maximum(old, x_ref[...])
        top_ref[...] = new
        scale = jnp.exp2(old - new)
        a_ref[...] = scale
        for lane in lanes:
            prob = jnp.exp2(tiles(s_ref[:, lane]) - new[None, :, lane])
            sum_ref[unit, :, lane] = sum_ref[unit, :, lane] * scale[:, lane] + jnp.sum(
                prob, axis=0
            )
            p_ref[:, lane] = prob.reshape(BLOCK, lane.stop - lane.start).astype(BF16)

    def gather(t, p_ref, a_ref):
        unit, key = unit_ref[t], key_ref[t]
        part = jnp.dot(vt_ref[key], p_ref[...], preferred_element_type=F32)
        kept = tiles(acc_ref[unit]) * a_ref[...][None]
        acc_ref[unit] = kept.reshape(HD, rows) + part

    def pair_step(i, _):
        t = LEAD + 2 * i
        gather(t - 2, p0, a0)
        weigh(t - 1, s1, x1, p1, a1)
        score(t, s0, x0)
        gather(t - 1, p1, a1)
        weigh(t, s0, x0, p0, a0)
        score(t + 1, s1, x1)
        return 0

    lax.fori_loop(0, (count_ref[0] + 1) // 2 + 1, pair_step, 0)

    def finish(unit, _):
        total = 1.0 / jnp.sum(sum_ref[unit], axis=0, keepdims=True)
        o_ref[unit] = (acc_ref[unit] * total).T.astype(BF16)
        return 0

    lax.fori_loop(0, units, finish, 0)


def attend(spot, jobs, q_pieces, v_pieces):
    groups = len(q_pieces)
    shards, spans, rows, _ = q_pieces[0].shape
    units, span = shards * spans, rows * groups
    nblk = units * span // BLOCK
    work = 3 * units
    scores = pltpu.VMEM((BLOCK, rows), F32)
    probs = pltpu.VMEM((BLOCK, rows), BF16)
    line = pltpu.VMEM((8, rows), F32)
    return pl.pallas_call(
        functools.partial(attend_kernel, groups),
        in_specs=[SMEM] * 4 + [HBM] * (2 * groups),
        out_specs=pl.BlockSpec(memory_space=pltpu.VMEM),
        out_shape=jax.ShapeDtypeStruct((units, rows, HD), BF16),
        scratch_shapes=[
            pltpu.VMEM((units, span, HD), BF16),
            pltpu.VMEM((units, span, HD), BF16),
            pltpu.VMEM((nblk, HD, BLOCK), BF16),
            pltpu.VMEM((nblk, BLOCK, HD), F32),
            *[scores, scores, line, line, probs, probs, line, line],
            line,
            pltpu.VMEM((units + 1, 8, rows), F32),
            pltpu.VMEM((units + 1, HD, rows), F32),
            pltpu.SemaphoreType.DMA,
            pltpu.SemaphoreType.DMA,
        ],
        cost_estimate=pl.CostEstimate(
            flops=4 * work * rows * BLOCK * HD,
            bytes_accessed=4 * units * span * HD,
            transcendentals=work * rows * BLOCK,
        ),
        name="attend",
    )(spot, *jobs, *q_pieces, *v_pieces)


def scores_kernel(groups, spot_ref, count_ref, unit_ref, key_ref, *refs):
    pieces = refs[:groups]
    p_out, scale_ref, q_ref, inv_ref, top_ref, p_buf, q_sem, p_sem = refs[groups : groups + 8]
    held = refs[groups + 8 :]
    s_refs, x_refs = held[:SCORE_STEP], held[SCORE_STEP:]
    shards, spans, rows, _ = pieces[0].shape
    units = shards * spans
    me = spot_ref[0]
    lanes = [slice(k, k + HD) for k in range(0, rows, HD)]

    def arrivals(s):
        some = pl.ds(s * spans, spans)
        return [
            pltpu.make_async_copy(
                pieces[r].at[s], q_ref.at[some, lax.rem(me + r, groups)], q_sem.at[s]
            )
            for r in range(groups)
        ]

    for s in range(shards):
        for copy in arrivals(s):
            copy.start()

    fold = math.log2(math.e) ** -2

    def prepare(s, _):
        for copy in arrivals(s):
            copy.wait()
        for k in range(spans * groups):
            unit, piece = s * spans + k // groups, k % groups
            wide = q_ref[unit, piece].astype(F32)
            total = jnp.sum(wide * wide, axis=1, keepdims=True)
            inv = lax.rsqrt(total * fold + 1e-06 * HD * fold)
            inv_ref[unit * groups + piece] = jnp.broadcast_to(inv, (BLOCK, HD))
        return 0

    lax.fori_loop(0, shards, prepare, 0)

    def tiles(x):
        return x.reshape(x.shape[0] // 8, 8, x.shape[1])

    def score(j, s_ref, x_ref):
        t = LEAD + j
        unit, key = jnp.minimum(unit_ref[t], units - 1), key_ref[t]
        first = unit_ref[t - 1] != unit_ref[t]
        gram = lax.dot_general(
            q_ref[key // groups, lax.rem(key, groups)],
            q_ref[unit, me],
            (((1,), (1,)), ((), ())),
            preferred_element_type=F32,
        )
        shift = jnp.where(first, 0, 2 * BLOCK)
        for lane in lanes:
            part = gram[:, lane] * inv_ref[key]
            band = part[lane]
            row = lax.broadcasted_iota(jnp.int32, band.shape, 0)
            col = lax.broadcasted_iota(jnp.int32, band.shape, 1)
            band = jnp.where(row - col == shift, NEG, band)
            above = [part[: lane.start]] if lane.start else []
            below = [part[lane.stop :]] if lane.stop < BLOCK else []
            part = jnp.concatenate(above + [band] + below, axis=0)
            s_ref[:, lane] = part
            most = jnp.max(jnp.max(tiles(part), axis=0), axis=0, keepdims=True)
            x_ref[:, lane] = jnp.broadcast_to(most, (8, HD))

    def weigh(j, s_ref, x_ref, slot, at):
        first = unit_ref[LEAD + j - 1] != unit_ref[LEAD + j]
        old = jnp.where(first, 2 * NEG, top_ref[...])
        new = jnp.maximum(old, x_ref[...])
        top_ref[...] = new
        scale_ref[pl.ds(j, 1), :] = jnp.exp2(old - new)[0:1]
        for lane in lanes:
            prob = jnp.exp2(tiles(s_ref[:, lane]) - new[None, :, lane])
            p_buf[slot, at, :, lane] = prob.reshape(BLOCK, HD).astype(BF16)

    def out_copy(chunk):
        slot = lax.rem(chunk, OUT_RING)
        return pltpu.make_async_copy(
            p_buf.at[slot], p_out.at[pl.ds(chunk * CHUNK, CHUNK)], p_sem.at[slot]
        )

    for i in range(SCORE_STEP):
        score(i, s_refs[i], x_refs[i])
    chunks = (count_ref[0] + CHUNK - 1) // CHUNK

    def chunk_step(chunk, _):
        slot = lax.rem(chunk, OUT_RING)

        @pl.when(chunk >= OUT_RING)
        def _():
            out_copy(chunk - OUT_RING).wait()

        def step(k, _):
            j = chunk * CHUNK + SCORE_STEP * k
            for i in range(SCORE_STEP):
                weigh(j + i, s_refs[i], x_refs[i], slot, SCORE_STEP * k + i)
            for i in range(SCORE_STEP):
                score(j + SCORE_STEP + i, s_refs[i], x_refs[i])
            return 0

        lax.fori_loop(0, CHUNK // SCORE_STEP, step, 0)
        out_copy(chunk).start()
        return 0

    lax.fori_loop(0, chunks, chunk_step, 0)
    for back in range(OUT_RING, 0, -1):

        @pl.when(chunks >= back)
        def _():
            out_copy(chunks - back).wait()


def attend_scores(spot, jobs, pieces):
    groups = len(pieces)
    shards, spans, rows, _ = pieces[0].shape
    units = shards * spans
    nblk = units * groups
    room = jobs[1].shape[0] // CHUNK * CHUNK
    work = 3 * units
    return pl.pallas_call(
        functools.partial(scores_kernel, groups),
        in_specs=[SMEM] * 4 + [HBM] * groups,
        out_specs=[HBM, pl.BlockSpec(memory_space=pltpu.VMEM)],
        out_shape=[
            jax.ShapeDtypeStruct((room, BLOCK, rows), BF16),
            jax.ShapeDtypeStruct((room, rows), F32),
        ],
        scratch_shapes=[
            pltpu.VMEM((units, groups, rows, HD), BF16),
            pltpu.VMEM((nblk, BLOCK, HD), F32),
            pltpu.VMEM((8, rows), F32),
            pltpu.VMEM((OUT_RING, CHUNK, BLOCK, rows), BF16),
            pltpu.SemaphoreType.DMA((shards,)),
            pltpu.SemaphoreType.DMA((OUT_RING,)),
            *[pltpu.VMEM((BLOCK, rows), F32)] * SCORE_STEP,
            *[pltpu.VMEM((8, rows), F32)] * SCORE_STEP,
        ],
        cost_estimate=pl.CostEstimate(
            flops=2 * work * rows * BLOCK * HD,
            bytes_accessed=2 * units * groups * rows * HD + 2 * work * rows * BLOCK,
            transcendentals=work * rows * BLOCK,
        ),
        name="attend_scores",
    )(spot, *jobs, *pieces)


def values_kernel(groups, spot_ref, count_ref, unit_ref, key_ref, *refs):
    pieces = refs[:groups]
    p_in, scale_in, o_out, acc_ref, p_buf, o_ref, scale_ref, p_sem, o_sem, scale_sem = refs[groups:]
    units, _, _ = pieces[0].shape
    me = spot_ref[0]
    chunks = (count_ref[0] + CHUNK - 1) // CHUNK

    def in_copy(chunk):
        slot = lax.rem(chunk, IN_RING)
        return pltpu.make_async_copy(
            p_in.at[pl.ds(chunk * CHUNK, CHUNK)], p_buf.at[slot], p_sem.at[slot]
        )

    scale_copy = pltpu.make_async_copy(scale_in, scale_ref, scale_sem)
    scale_copy.start()
    for ahead in range(IN_RING - 1):

        @pl.when(ahead < chunks)
        def _():
            in_copy(ahead).start()

    def clear(unit, _):
        acc_ref[unit] = jnp.zeros(acc_ref.shape[1:], F32)
        return 0

    lax.fori_loop(0, units + 1, clear, 0)
    scale_copy.wait()
    ones = jnp.ones((ONES, BLOCK), BF16)

    def gather(j, prob):
        unit, key = unit_ref[LEAD + j], key_ref[LEAD + j]
        source = lax.rem(key + groups - me, groups)
        turned = pieces[0][key // groups]
        for r in range(1, groups):
            turned = jnp.where(source == r, pieces[r][key // groups], turned)
        part = jnp.dot(
            jnp.concatenate([turned, ones], axis=0), prob, preferred_element_type=F32
        )
        acc_ref[unit] = acc_ref[unit] * scale_ref[pl.ds(j, 1), :] + part[: HD + 8]

    def chunk_step(chunk, _):
        slot = lax.rem(chunk, IN_RING)

        @pl.when(chunk + IN_RING - 1 < chunks)
        def _():
            in_copy(chunk + IN_RING - 1).start()

        in_copy(chunk).wait()

        def step(k, _):
            for i in range(VALUE_STEP):
                at = VALUE_STEP * k + i
                gather(chunk * CHUNK + at, p_buf[slot, at])
            return 0

        lax.fori_loop(0, CHUNK // VALUE_STEP, step, 0)
        return 0

    lax.fori_loop(0, chunks, chunk_step, 0)

    def result(i):
        some = pl.ds(i * FINISH_STEP, FINISH_STEP)
        return pltpu.make_async_copy(o_ref.at[some], o_out.at[some], o_sem.at[i])

    def finish(i, _):
        for k in range(FINISH_STEP):
            unit = i * FINISH_STEP + k
            inverse = 1.0 / acc_ref[unit, HD : HD + 1, :]
            o_ref[unit] = (acc_ref[unit, 0:HD, :] * inverse).astype(BF16).T
        result(i).start()
        return 0

    lax.fori_loop(0, units // FINISH_STEP, finish, 0)
    for i in range(units // FINISH_STEP):
        result(i).wait()


def attend_values(spot, jobs, pieces, probs, scales):
    groups = len(pieces)
    shards, spans, _, rows = pieces[0].shape
    units = shards * spans
    work = 3 * units
    vmem = pl.BlockSpec(memory_space=pltpu.VMEM)
    pieces = [
        pltpu.with_memory_space_constraint(x.reshape(units, HD, rows), pltpu.VMEM)
        for x in pieces
    ]
    return pl.pallas_call(
        functools.partial(values_kernel, groups),
        in_specs=[SMEM] * 4 + [vmem] * groups + [HBM] * 2,
        out_specs=pl.BlockSpec(memory_space=pltpu.HBM),
        out_shape=pltpu.HBM((units, rows, HD), BF16),
        scratch_shapes=[
            pltpu.VMEM((units + 1, HD + 8, rows), F32),
            pltpu.VMEM((IN_RING, CHUNK, BLOCK, rows), BF16),
            pltpu.VMEM((units, rows, HD), BF16),
            pltpu.VMEM(scales.shape, F32),
            pltpu.SemaphoreType.DMA((IN_RING,)),
            pltpu.SemaphoreType.DMA((units // FINISH_STEP,)),
            pltpu.SemaphoreType.DMA,
        ],
        compiler_params=pltpu.CompilerParams(vmem_limit_bytes=24 * MIB),
        cost_estimate=pl.CostEstimate(
            flops=2 * work * rows * BLOCK * HD,
            bytes_accessed=2 * units * groups * rows * HD + 2 * work * rows * BLOCK,
            transcendentals=0,
        ),
        name="attend_values",
    )(spot, *jobs, *pieces, probs, pltpu.with_memory_space_constraint(scales, pltpu.HBM))


def group_shift(x, shards, groups, r):
    pairs = [(i - i % groups + (i % groups + r) % groups, i) for i in range(shards)]
    return lax.ppermute(x, "seq", pairs)


def ring_weights(w_out, groups, member):
    count = lax.axis_size("head")
    here = lax.axis_index("head")
    share = w_out.shape[0] // groups
    up = down = lax.dynamic_slice_in_dim(w_out, member * share, share, 0)
    ups, downs = {}, {}
    for k in range(1, count):
        up = lax.ppermute(up, "head", [(i, i + 1) for i in range(k - 1, count - 1)])
        down = lax.ppermute(down, "head", [(i, i - 1) for i in range(1, count - k + 1)])
        ups[k], downs[k] = up, down
    return [
        jnp.where(here + r < count, downs[r], ups[count - r]) for r in range(1, count)
    ]


def project_kernel(spot_ref, x_ref, w_ref, *refs):
    heads, groups, spans, rows, _ = x_ref.shape
    pieces = refs[: (spans - 1) * groups]
    o_ref, wide_ref, w_buf, sem = refs[(spans - 1) * groups :]
    member, z = spot_ref[0], spot_ref[1]
    tile = w_buf.shape[2]
    share = pieces[0].shape[0]
    depth = heads * HD
    step = pl.program_id(0)

    def copies(slot):
        cols = pl.ds(slot * tile, tile)
        if not isinstance(slot, int):
            cols = pl.ds(pl.multiple_of(slot * tile, tile), tile)
        out = [
            pltpu.make_async_copy(
                w_ref.at[:, cols],
                w_buf.at[slot, pl.ds(pl.multiple_of(z * depth, depth), depth), :],
                sem.at[slot],
            )
        ]
        for r in range(1, spans):
            for k in range(groups):
                at = lax.rem(z + r, spans) * depth + lax.rem(member + k, groups) * share
                out.append(
                    pltpu.make_async_copy(
                        pieces[(r - 1) * groups + k].at[:, cols],
                        w_buf.at[slot, pl.ds(pl.multiple_of(at, share), share), :],
                        sem.at[slot],
                    )
                )
        return out

    @pl.when(step == 0)
    def _():
        for i in range(w_buf.shape[0]):
            for copy in copies(i):
                copy.start()
        for z_at in range(spans):
            for h in range(heads):
                at = (z_at * heads + h) * HD
                for g in range(groups):
                    wide_ref[g * rows : (g + 1) * rows, at : at + HD] = x_ref[h, g, z_at]

    for copy in copies(step):
        copy.wait()
    o_ref[...] = jnp.dot(wide_ref[...], w_buf[step], preferred_element_type=F32).astype(BF16)


def project(spot, mixed, w_out, pieces):
    _, groups, spans, rows, _ = mixed.shape
    depth, width = w_out.shape
    tile = min(PROJECT_TILE, width)
    out_rows = groups * rows
    return pl.pallas_call(
        project_kernel,
        grid=(width // tile,),
        in_specs=[SMEM, pl.BlockSpec(memory_space=pltpu.VMEM)] + [HBM] * (1 + len(pieces)),
        out_specs=pl.BlockSpec((out_rows, tile), lambda i: (0, i)),
        out_shape=jax.ShapeDtypeStruct((out_rows, width), BF16),
        scratch_shapes=[
            pltpu.VMEM((out_rows, spans * depth), BF16),
            pltpu.VMEM((width // tile, spans * depth, tile), BF16),
            pltpu.SemaphoreType.DMA((width // tile,)),
        ],
        cost_estimate=pl.CostEstimate(
            flops=2 * out_rows * spans * depth * width,
            bytes_accessed=2 * spans * depth * width,
            transcendentals=0,
        ),
        name="project",
    )(spot, pltpu.with_memory_space_constraint(mixed, pltpu.VMEM), w_out, *pieces)


def body(qk, values, bucket, pair_row, pair_col, pair_count, w_out):
    shards = lax.axis_size("seq")
    spans = lax.axis_size("head")
    tokens, width = qk.shape
    heads = width // HD
    groups = shards // heads
    blocks = tokens // BLOCK
    slots = pair_row.shape[2]
    here, z = lax.axis_index("seq"), lax.axis_index("head")
    head, member = here // groups, lax.rem(here, groups)
    spot = jnp.stack([member, z, here, z * heads + head]).astype(jnp.int32)

    shares = ring_weights(w_out, groups, member)
    units = shards * spans
    rows = tokens // spans // groups
    turned = rows == BLOCK

    def send(x, turn):
        sent = pack(x, spans, groups, turn)
        sent = sent.reshape(shards, spans, *sent.shape[3:])
        got = lax.all_to_all(sent, "seq", 0, 0, tiled=True)
        return [got] + [group_shift(got, shards, groups, r) for r in range(1, groups)]

    q_pieces = send(qk, False)
    v_pieces = send(values, turned)
    tables = gather_tables(pair_row, pair_col, pair_count, shards)
    jobs = job_lists(
        tables, bucket, spot, shards, slots, blocks, units, tokens // spans, rows
    )
    if turned:
        weights = attend_scores(spot, jobs, q_pieces)
        attn = attend_values(spot, jobs, v_pieces, *weights)
    else:
        attn = attend(spot, jobs, q_pieces, v_pieces)
    mixed = lax.all_to_all(attn, ("seq", "head"), 0, 0, tiled=True)
    mixed = mixed.reshape(heads, groups, spans, rows, HD)
    weights = []
    shares = [pltpu.with_memory_space_constraint(x, pltpu.HBM) for x in shares]
    for piece in shares:
        weights += [piece] + [
            group_shift(piece, shards, groups, k) for k in range(1, groups)
        ]
    weights = [pltpu.with_memory_space_constraint(x, pltpu.HBM) for x in weights]
    return project(spot, mixed, w_out, weights)


def solution(mesh):
    return jax.shard_map(
        body,
        mesh=mesh,
        in_specs=(
            P("seq", "head"),
            P("seq", "head"),
            P(),
            P("seq", None, None),
            P("seq", None, None),
            P("seq", None),
            P("head", None),
        ),
        out_specs=P(("seq", "head"), None),
        check_vma=False,
    )
```
